32 devices in a mesh: dp: 8 (over y, x, core), tensor: 4 (over z).
Axes of the slice: x: 2, y: 2, z: 4, core: 2. Of those that a mesh axis runs over, the one named last changes fastest.
Arguments:
- inputs_x: bfloat16 [1024, 4096], P('dp', 'tensor'), may hold values from -6 to 6
- hidden: bfloat16 [1024, 14336], P('dp', 'tensor'), may hold values from -6 to 6
- grad_up: bfloat16 [1024, 14336], P('dp', 'tensor'), may hold values from -6 to 6
- grad_down: bfloat16 [1024, 4096], P('dp', 'tensor'), may hold values from -6 to 6
- proj_in_up: bfloat16 [4096, 64], P('tensor'), may hold values from -0.09375 to 0.09375
- proj_in_down: bfloat16 [14336, 64], P('tensor'), may hold values from -0.046875 to 0.046875
- proj_out_up: bfloat16 [14336, 64], P('tensor'), may hold values from -0.046875 to 0.046875
- proj_out_down: bfloat16 [4096, 64], P('tensor'), may hold values from -0.09375 to 0.09375
- lengths: int32 [16], P('dp'), may hold values from 16 to 64
- stored_grads: bfloat16 [208, 8192], P('dp', 'tensor'), may hold values from -6 to 6
Outputs:
- gram: bfloat16 [8192, 8, 1024], P('tensor', 'dp')
The draws below stay inside these ranges and needn't reach their ends.
All inputs are finite; a program needn't handle non-finite values.
Results may differ from the reference program's by a relative error of at most 0.0034.
Values may be sent and summed in bfloat16 or wider, within the bound.
No kernel may reach another device: no remote copies, remote signals or barrier semaphores. Data moves between devices by JAX's collectives and lax.ppermute only.
A program may use at most 64 MiB of HBM per device.

```python
import math
import jax
import jax.numpy as jnp
from jax import lax

D = 4096
FF = 14336
K = 64
LAYERS = 2
SLOTS = 64
EXAMPLES = 16
TOKENS = 1024
STORED = 208
FEAT = 8192
N_DP = 8
N_TENSOR = 4


def place_ends(entries, own_key, smallest, largest):
    place = [jax.random.randint(jax.random.fold_in(own_key, axis), (), 0, length) for axis, length in enumerate(entries.shape)]
    widest = entries.shape.index(max(entries.shape))
    beside = place[:widest] + [(place[widest] + 1) % entries.shape[widest]] + place[widest + 1:]
    return entries.at[tuple(place)].set(smallest).at[tuple(beside)].set(largest)


def block_scale(rng, extent, cuts, low, top_value):
    def one(axis_at, shards_of):
        steps = jax.random.uniform(jax.random.fold_in(jax.random.fold_in(rng, 6), axis_at), (shards_of,), jnp.float32, low / len(cuts), top_value / len(cuts))
        return jnp.repeat(jnp.exp(steps), extent[axis_at] // shards_of).reshape((-1,) + (1,) * (len(extent) - axis_at - 1))

    loudness = one(*cuts[0])
    for cut in cuts[1:]:
        loudness = loudness * one(*cut)
    return loudness


def noise(own_key, extent, deviation, reach, pieces=(), kind=jnp.bfloat16):
    drawn = deviation * jax.random.normal(own_key, extent, jnp.float32)
    if pieces:
        drawn = drawn * block_scale(own_key, extent, pieces, -0.22, 0.18)
    return jnp.clip(drawn, -reach, reach).astype(kind)


def setup_inputs(seed: int = 0) -> dict:
    key_list = jax.random.split(jax.random.key(seed), 11)
    inputs_x = noise(key_list[0], (TOKENS, D), 1.0, 6.0, ((0, 8), (1, 4)))
    hidden = noise(key_list[1], (TOKENS, FF), 1.0, 6.0, ((0, 8), (1, 4)))
    grad_up = noise(key_list[2], (TOKENS, FF), 1.0, 6.0, ((0, 8), (1, 4)))
    grad_down = noise(key_list[3], (TOKENS, D), 1.0, 6.0, ((0, 8), (1, 4)))
    proj_in_up = noise(key_list[4], (D, K), D ** -0.5, 0.09375, ((0, 4),))
    proj_in_down = noise(key_list[5], (FF, K), FF ** -0.5, 0.046875, ((0, 4),))
    proj_out_up = noise(key_list[6], (FF, K), FF ** -0.5, 0.046875, ((0, 4),))
    proj_out_down = noise(key_list[7], (D, K), D ** -0.5, 0.09375, ((0, 4),))
    lengths = place_ends(jax.random.randint(key_list[8], (EXAMPLES,), SLOTS // 4, SLOTS + 1), jax.random.fold_in(key_list[8], 1), SLOTS // 4, SLOTS).astype(jnp.int32)
    stored_grads = noise(key_list[9], (STORED, FEAT), 1.0, 6.0, ((0, 8), (1, 4)))
    return {"inputs_x": inputs_x, "hidden": hidden, "grad_up": grad_up, "grad_down": grad_down, "proj_in_up": proj_in_up, "proj_in_down": proj_in_down, "proj_out_up": proj_out_up, "proj_out_down": proj_out_down, "lengths": lengths, "stored_grads": stored_grads}


def matmul(left, right):
    return jnp.dot(left, right, preferred_element_type=jnp.float32)

def reference(inputs_x, hidden, grad_up, grad_down, proj_in_up, proj_in_down, proj_out_up, proj_out_down, lengths, stored_grads):
    examples = lengths.shape[0]
    live_mask = (jnp.arange(SLOTS, dtype=jnp.int32)[None, :] < lengths[:, None]).astype(jnp.float32)
    in_proj = jnp.stack([matmul(inputs_x, proj_in_up), matmul(hidden, proj_in_down)], axis=1)
    out_proj = jnp.stack([matmul(grad_up, proj_out_up), matmul(grad_down, proj_out_down)], axis=1)
    in_proj = in_proj.reshape(examples, SLOTS, LAYERS, K)
    out_proj = out_proj.reshape(examples, SLOTS, LAYERS, K) * live_mask[:, :, None, None]
    current = jnp.einsum('esla,eslb->ealb', out_proj, in_proj, precision=lax.Precision.HIGHEST)
    current = (current * (1.0 / math.sqrt(SLOTS))).reshape(examples, FEAT).astype(jnp.bfloat16)
    rows = jnp.concatenate([current, stored_grads], axis=0)
    full = lax.dot_general(rows, rows, (((0,), (0,)), ((), ())), preferred_element_type=jnp.float32)
    full = full * (1.0 / math.sqrt(rows.shape[0]))
    quarter = FEAT // N_TENSOR
    sub_width = quarter // N_DP
    gram = full.reshape(FEAT, N_TENSOR, N_DP, sub_width).transpose(0, 2, 1, 3)
    return gram.reshape(FEAT, N_DP, N_TENSOR * sub_width).astype(jnp.bfloat16)
```

```python
import functools
import math

import jax
import jax.numpy as jnp
from jax import lax
from jax.experimental import pallas as pl
from jax.experimental.pallas import tpu as pltpu
from jax.sharding import PartitionSpec as P

LAYERS = 2
LANES = 128
SLOT = 16


def matmul(left, right):
    return jnp.dot(left, right, preferred_element_type=jnp.float32)


def power_of_two(n):
    return n & (n - 1) == 0


def bits_of(n):
    return [1 << k for k in range(n.bit_length() - 1)]


def swap(value, axis, bit):
    count = lax.axis_size(axis)
    return lax.ppermute(value, axis, [(i, i ^ bit) for i in range(count)])


def project_kernel(x, h, gu, gd, pu, pd, ou, od, out, *scratch):
    ins = (x, h, gu, gd, pu, pd, ou, od)
    bufs, sem = scratch[:8], scratch[8]
    order = (4, 0, 7, 3, 5, 1, 6, 2)
    copies = {}
    for n in order:
        copies[n] = pltpu.make_async_copy(ins[n], bufs[n], sem.at[n])
        copies[n].start()

    def product(left, right):
        copies[right].wait()
        copies[left].wait()
        return lax.dot_general(
            bufs[left][...],
            bufs[right][...],
            (((1,), (1,)), ((), ())),
            preferred_element_type=jnp.float32,
        )

    rows = x.shape[0]
    in_up = product(0, 4)
    out_down = product(3, 7)
    in_down = product(1, 5)
    out[:rows, :] = jnp.concatenate([in_up, in_down], axis=1)
    out_up = product(2, 6)
    out[rows:, :] = jnp.concatenate([out_up, out_down], axis=1)


def project(x, h, gu, gd, pu, pd, ou, od):
    args = (x, h, gu, gd, pu.T, pd.T, ou.T, od.T)
    rows = x.shape[0]
    width = LAYERS * pu.shape[1]
    return pl.pallas_call(
        project_kernel,
        out_shape=jax.ShapeDtypeStruct((2 * rows, width), jnp.float32),
        in_specs=[pl.BlockSpec(memory_space=pl.ANY)] * 8,
        out_specs=pl.BlockSpec(memory_space=pltpu.VMEM),
        scratch_shapes=[pltpu.VMEM(a.shape, a.dtype) for a in args]
        + [pltpu.SemaphoreType.DMA((8,))],
        cost_estimate=pl.CostEstimate(
            flops=2 * sum(math.prod(a.shape) for a in args[:4]) * pu.shape[1],
            bytes_accessed=2 * sum(math.prod(a.shape) for a in args),
            transcendentals=0,
        ),
        name="project",
    )(*args)


def current_kernel(lengths, own, other, out):
    examples, half, width = out.shape
    total = own[...] + other[...]
    rows = total.shape[0] // 2
    slots = rows // examples
    position = lax.broadcasted_iota(jnp.int32, (slots, width), 0)
    lane = lax.broadcasted_iota(jnp.int32, (half, width), 1)
    for e in range(examples):
        left = total[rows + e * slots : rows + (e + 1) * slots]
        right = total[e * slots : (e + 1) * slots]
        left = left * (position < lengths[e]).astype(jnp.float32)
        both = lax.dot_general(
            left,
            right,
            (((0,), (0,)), ((), ())),
            precision=lax.Precision.HIGHEST,
            preferred_element_type=jnp.float32,
        )
        mine = jnp.where(lane < half, both[:half], both[half:])
        out[e] = (mine * (1.0 / math.sqrt(slots))).astype(out.dtype)


def current_rows(lengths, own, other, proj_width):
    examples = lengths.shape[0]
    return pl.pallas_call(
        current_kernel,
        out_shape=jax.ShapeDtypeStruct(
            (examples, proj_width, LAYERS * proj_width), jnp.bfloat16
        ),
        in_specs=[
            pl.BlockSpec(memory_space=pltpu.SMEM),
            pl.BlockSpec(memory_space=pltpu.VMEM),
            pl.BlockSpec(memory_space=pltpu.VMEM),
        ],
        out_specs=pl.BlockSpec(memory_space=pltpu.VMEM),
        cost_estimate=pl.CostEstimate(
            flops=2 * examples * 64 * width_flops(proj_width),
            bytes_accessed=own.size * 8,
            transcendentals=0,
        ),
        name="current",
    )(lengths, own, other)


def width_flops(proj_width):
    return (LAYERS * proj_width) ** 2


def gram_kernel(scale, offsets, place, stored, cols, cur, out, left, right, buf, sem):
    pieces, old, quarter = stored.shape
    new = cur.shape[1]
    sub = cols.shape[-1]
    slot = left.shape[0] // pieces
    q, i = place[0], place[1]
    left[...] = jnp.zeros_like(left)
    right[...] = jnp.zeros_like(right)
    for p in range(pieces):
        left[p * slot : p * slot + old, :] = stored[p]
        left[p * slot + old : p * slot + old + new, :] = cur[
            p, :, pl.ds(pl.multiple_of(q * quarter, quarter), quarter)
        ]
    for k, off in enumerate(offsets):
        to = pl.multiple_of((q ^ off) * sub, sub)
        source = pl.multiple_of((q ^ off) * quarter + i * sub, sub)
        for p in range(pieces):
            right[p * slot : p * slot + old, pl.ds(to, sub)] = cols[k, p]
            right[p * slot + old : p * slot + old + new, pl.ds(to, sub)] = cur[
                p, :, pl.ds(source, sub)
            ]
    chunk = buf.shape[1]
    copies = []
    for m in range(buf.shape[0]):
        product = lax.dot_general(
            left[:, m * chunk : (m + 1) * chunk],
            right[...],
            (((0,), (0,)), ((), ())),
            preferred_element_type=jnp.float32,
        )
        buf[m] = (product * scale).astype(buf.dtype)
        copies.append(
            pltpu.make_async_copy(
                buf.at[m], out.at[pl.ds(m * chunk, chunk)], sem.at[m]
            )
        )
        copies[-1].start()
    for copy in copies:
        copy.wait()


def gram(stored, cols, cur, place, offsets):
    pieces, old, quarter = stored.shape
    new = cur.shape[1]
    slot = -(-(old + new) // SLOT) * SLOT
    width = cols.shape[0] * cols.shape[-1]
    chunk = 256 if quarter % 256 == 0 else quarter
    scale = 1.0 / math.sqrt(pieces * (old + new))
    return pl.pallas_call(
        functools.partial(gram_kernel, scale, offsets),
        out_shape=jax.ShapeDtypeStruct((quarter, width), jnp.bfloat16),
        in_specs=[pl.BlockSpec(memory_space=pltpu.SMEM)]
        + [pl.BlockSpec(memory_space=pltpu.VMEM)] * 3,
        out_specs=pl.BlockSpec(memory_space=pl.ANY),
        scratch_shapes=[
            pltpu.VMEM((pieces * slot, quarter), jnp.bfloat16),
            pltpu.VMEM((pieces * slot, width), jnp.bfloat16),
            pltpu.VMEM((quarter // chunk, chunk, width), jnp.bfloat16),
            pltpu.SemaphoreType.DMA((quarter // chunk,)),
        ],
        cost_estimate=pl.CostEstimate(
            flops=2 * pieces * slot * quarter * width,
            bytes_accessed=2 * quarter * width,
            transcendentals=0,
        ),
        name="gram",
    )(place, stored, cols, cur)


def local(
    inputs_x,
    hidden,
    grad_up,
    grad_down,
    proj_in_up,
    proj_in_down,
    proj_out_up,
    proj_out_down,
    lengths,
    stored_grads,
):
    examples = lengths.shape[0]
    proj_width = proj_in_up.shape[1]
    quarter = stored_grads.shape[1]
    dp_count = lax.axis_size("dp")
    tensor_count = lax.axis_size("tensor")
    sub_width = quarter // dp_count
    q, i = lax.axis_index("tensor"), lax.axis_index("dp")
    dp_bits = bits_of(dp_count)
    tensor_bits = bits_of(tensor_count)

    partial = project(
        inputs_x,
        hidden,
        grad_up,
        grad_down,
        proj_in_up,
        proj_in_down,
        proj_out_up,
        proj_out_down,
    )
    rows = stored_grads[None]
    for bit in dp_bits[1:] + dp_bits[:1]:
        rows = jnp.concatenate([rows, swap(rows, "dp", bit)], axis=0)
    cols = lax.dynamic_slice_in_dim(rows, i * sub_width, sub_width, 2)[None]
    offsets = [0]
    for bit in reversed(tensor_bits):
        cols = jnp.concatenate([cols, swap(cols, "tensor", bit)], axis=0)
        offsets += [off ^ bit for off in offsets]

    total = partial
    for bit in tensor_bits[:-1]:
        total = total + swap(total, "tensor", bit)
    other = swap(total, "tensor", tensor_bits[-1])
    cur = current_rows(lengths, total, other, proj_width)
    cur = cur.reshape(1, examples, proj_width * LAYERS * proj_width)
    for bit in reversed(dp_bits):
        cur = jnp.concatenate([cur, swap(cur, "dp", bit)], axis=0)
    place = jnp.stack([q, i]).astype(jnp.int32)
    product = gram(rows, cols, cur, place, offsets)
    return product.reshape(quarter, 1, tensor_count * sub_width)


def local_any(
    inputs_x,
    hidden,
    grad_up,
    grad_down,
    proj_in_up,
    proj_in_down,
    proj_out_up,
    proj_out_down,
    lengths,
    stored_grads,
):
    examples = lengths.shape[0]
    slot_count = inputs_x.shape[0] // examples
    proj_width = proj_in_up.shape[1]
    tensor_count = lax.axis_size("tensor")
    out_share = proj_width // tensor_count
    tensor_index = lax.axis_index("tensor")
    terms_in = jnp.stack([matmul(inputs_x, proj_in_up), matmul(hidden, proj_in_down)])
    terms_out = jnp.stack([matmul(grad_up, proj_out_up), matmul(grad_down, proj_out_down)])
    summed_in, summed_out = lax.psum((terms_in, terms_out), "tensor")
    summed_out = lax.dynamic_slice_in_dim(summed_out, tensor_index * out_share, out_share, 2)
    live_mask = (jnp.arange(slot_count, dtype=jnp.int32)[None, :] < lengths[:, None]).astype(
        jnp.float32
    )
    in_proj = summed_in.reshape(LAYERS, examples, slot_count, proj_width).transpose(1, 2, 0, 3)
    out_proj = summed_out.reshape(LAYERS, examples, slot_count, out_share).transpose(1, 2, 0, 3)
    out_proj = out_proj * live_mask[:, :, None, None]
    current = jnp.einsum("esla,eslb->ealb", out_proj, in_proj, precision=lax.Precision.HIGHEST)
    current = (current * (1.0 / math.sqrt(slot_count))).reshape(
        examples, out_share * LAYERS * proj_width
    )
    local_rows = jnp.concatenate([current.astype(jnp.bfloat16), stored_grads], axis=0)
    row_count = local_rows.shape[0]
    quarter = local_rows.shape[1]
    dp_count = lax.axis_size("dp")
    sub_width = quarter // dp_count
    every_count = row_count * dp_count
    everything = lax.all_gather(local_rows, "dp", axis=0, tiled=True)
    column_block = lax.dynamic_slice_in_dim(
        everything, lax.axis_index("dp") * sub_width, sub_width, 1
    )
    columns = lax.all_gather(column_block, "tensor", axis=1, tiled=True)
    product = lax.dot_general(
        everything, columns, (((0,), (0,)), ((), ())), preferred_element_type=jnp.float32
    )
    product = product * (1.0 / math.sqrt(every_count))
    return product.astype(jnp.bfloat16).reshape(quarter, 1, columns.shape[1])


def paired(dp_count, tensor_count, proj_width, quarter):
    sizes = power_of_two(dp_count) and power_of_two(tensor_count)
    many = dp_count > 1 and tensor_count > 1
    lanes = quarter % (dp_count * LANES) == 0 and LAYERS * proj_width == LANES
    return sizes and many and lanes


def solution(mesh):
    in_specs = (
        P("dp", "tensor"),
        P("dp", "tensor"),
        P("dp", "tensor"),
        P("dp", "tensor"),
        P("tensor", None),
        P("tensor", None),
        P("tensor", None),
        P("tensor", None),
        P("dp"),
        P("dp", "tensor"),
    )
    out_specs = P("tensor", "dp", None)

    def step(*args):
        counts = mesh.shape["dp"], mesh.shape["tensor"]
        quarter = args[9].shape[1] // counts[1]
        fits = paired(*counts, args[4].shape[1], quarter)
        body = local if fits else local_any
        return jax.shard_map(
            body, mesh=mesh, in_specs=in_specs, out_specs=out_specs, check_vma=False
        )(*args)

    return step
```

```python
import functools
import math

import jax
import jax.numpy as jnp
from jax import lax
from jax.experimental import pallas as pl
from jax.experimental.pallas import tpu as pltpu
from jax.sharding import PartitionSpec as P

LAYERS = 2
LANES = 128
SLOT = 16
MIB = 1 << 20


def matmul(left, right):
    return jnp.dot(left, right, preferred_element_type=jnp.float32)


def power_of_two(n):
    return n & (n - 1) == 0


def bits_of(n):
    return [1 << k for k in range(n.bit_length() - 1)]


def swap(value, axis, bit):
    count = lax.axis_size(axis)
    return lax.ppermute(value, axis, [(i, i ^ bit) for i in range(count)])


def project_kernel(x, h, gu, gd, pu, pd, ou, od, out, *scratch):
    ins = (x, h, gu, gd, pu, pd, ou, od)
    bufs, sem = scratch[:8], scratch[8]
    order = (4, 0, 7, 3, 5, 1, 6, 2)
    copies = {}
    for n in order:
        copies[n] = pltpu.make_async_copy(ins[n], bufs[n], sem.at[n])
        copies[n].start()

    def product(left, right):
        copies[right].wait()
        copies[left].wait()
        return lax.dot_general(
            bufs[left][...],
            bufs[right][...],
            (((1,), (1,)), ((), ())),
            preferred_element_type=jnp.float32,
        )

    rows = x.shape[0]
    in_up = product(0, 4)
    out_down = product(3, 7)
    in_down = product(1, 5)
    out[:rows, :] = jnp.concatenate([in_up, in_down], axis=1)
    out_up = product(2, 6)
    out[rows:, :] = jnp.concatenate([out_up, out_down], axis=1)


def project(x, h, gu, gd, pu, pd, ou, od):
    args = (x, h, gu, gd, pu.T, pd.T, ou.T, od.T)
    args = tuple(pltpu.with_memory_space_constraint(a, pltpu.HBM) for a in args)
    rows = x.shape[0]
    width = LAYERS * pu.shape[1]
    return pl.pallas_call(
        project_kernel,
        out_shape=jax.ShapeDtypeStruct((2 * rows, width), jnp.float32),
        in_specs=[pl.BlockSpec(memory_space=pltpu.HBM)] * 8,
        out_specs=pl.BlockSpec(memory_space=pltpu.VMEM),
        scratch_shapes=[pltpu.VMEM(a.shape, a.dtype) for a in args]
        + [pltpu.SemaphoreType.DMA((8,))],
        cost_estimate=pl.CostEstimate(
            flops=2 * sum(math.prod(a.shape) for a in args[:4]) * pu.shape[1],
            bytes_accessed=2 * sum(math.prod(a.shape) for a in args),
            transcendentals=0,
        ),
        compiler_params=pltpu.CompilerParams(vmem_limit_bytes=8 * MIB),
        name="project",
    )(*args)


def current_kernel(lengths, own, other, out):
    examples, half, width = out.shape
    total = own[...] + other[...]
    rows = total.shape[0] // 2
    slots = rows // examples
    position = lax.broadcasted_iota(jnp.int32, (slots, width), 0)
    lane = lax.broadcasted_iota(jnp.int32, (half, width), 1)
    for e in range(examples):
        left = total[rows + e * slots : rows + (e + 1) * slots]
        right = total[e * slots : (e + 1) * slots]
        left = left * (position < lengths[e]).astype(jnp.float32)
        both = lax.dot_general(
            left,
            right,
            (((0,), (0,)), ((), ())),
            precision=lax.Precision.HIGHEST,
            preferred_element_type=jnp.float32,
        )
        mine = jnp.where(lane < half, both[:half], both[half:])
        out[e] = (mine * (1.0 / math.sqrt(slots))).astype(out.dtype)


def current_rows(lengths, own, other, proj_width):
    examples = lengths.shape[0]
    return pl.pallas_call(
        current_kernel,
        out_shape=jax.ShapeDtypeStruct(
            (examples, proj_width, LAYERS * proj_width), jnp.bfloat16
        ),
        in_specs=[
            pl.BlockSpec(memory_space=pltpu.SMEM),
            pl.BlockSpec(memory_space=pltpu.VMEM),
            pl.BlockSpec(memory_space=pltpu.VMEM),
        ],
        out_specs=pl.BlockSpec(memory_space=pltpu.VMEM),
        cost_estimate=pl.CostEstimate(
            flops=2 * examples * 64 * width_flops(proj_width),
            bytes_accessed=own.size * 8,
            transcendentals=0,
        ),
        compiler_params=pltpu.CompilerParams(vmem_limit_bytes=4 * MIB),
        name="current",
    )(lengths, own, other)


def width_flops(proj_width):
    return (LAYERS * proj_width) ** 2


def gram_kernel(scale, offsets, stored, cols, cur, out, left, right, buf, sem):
    pieces, old, quarter = stored.shape
    new = cur.shape[1]
    sub = cols.shape[-1]
    slot = left.shape[0] // pieces
    q, i = lax.axis_index("tensor"), lax.axis_index("dp")
    left[...] = jnp.zeros_like(left)
    right[...] = jnp.zeros_like(right)
    for p in range(pieces):
        left[p * slot : p * slot + old, :] = stored[p]
        left[p * slot + old : p * slot + old + new, :] = cur[
            p, :, pl.ds(pl.multiple_of(q * quarter, quarter), quarter)
        ]
    for k, off in enumerate(offsets):
        to = pl.multiple_of((q ^ off) * sub, sub)
        source = pl.multiple_of((q ^ off) * quarter + i * sub, sub)
        for p in range(pieces):
            right[p * slot : p * slot + old, pl.ds(to, sub)] = cols[k, p]
            right[p * slot + old : p * slot + old + new, pl.ds(to, sub)] = cur[
                p, :, pl.ds(source, sub)
            ]
    chunk = buf.shape[1]
    copies = []
    for m in range(buf.shape[0]):
        product = lax.dot_general(
            left[:, m * chunk : (m + 1) * chunk],
            right[...],
            (((0,), (0,)), ((), ())),
            preferred_element_type=jnp.float32,
        )
        buf[m] = (product * scale).astype(buf.dtype)
        copies.append(
            pltpu.make_async_copy(
                buf.at[m], out.at[pl.ds(m * chunk, chunk)], sem.at[m]
            )
        )
        copies[-1].start()
    for copy in copies:
        copy.wait()


def gram(stored, cols, cur, offsets):
    pieces, old, quarter = stored.shape
    new = cur.shape[1]
    slot = -(-(old + new) // SLOT) * SLOT
    width = cols.shape[0] * cols.shape[-1]
    chunk = 256 if quarter % 256 == 0 else quarter
    scale = 1.0 / math.sqrt(pieces * (old + new))
    return pl.pallas_call(
        functools.partial(gram_kernel, scale, offsets),
        out_shape=jax.ShapeDtypeStruct((quarter, width), jnp.bfloat16),
        in_specs=[pl.BlockSpec(memory_space=pltpu.VMEM)] * 3,
        out_specs=pl.BlockSpec(memory_space=pltpu.HBM),
        scratch_shapes=[
            pltpu.VMEM((pieces * slot, quarter), jnp.bfloat16),
            pltpu.VMEM((pieces * slot, width), jnp.bfloat16),
            pltpu.VMEM((quarter // chunk, chunk, width), jnp.bfloat16),
            pltpu.SemaphoreType.DMA((quarter // chunk,)),
        ],
        cost_estimate=pl.CostEstimate(
            flops=2 * pieces * slot * quarter * width,
            bytes_accessed=2 * quarter * width,
            transcendentals=0,
        ),
        compiler_params=pltpu.CompilerParams(vmem_limit_bytes=24 * MIB),
        name="gram",
    )(stored, cols, cur)


def local(
    inputs_x,
    hidden,
    grad_up,
    grad_down,
    proj_in_up,
    proj_in_down,
    proj_out_up,
    proj_out_down,
    lengths,
    stored_grads,
):
    examples = lengths.shape[0]
    proj_width = proj_in_up.shape[1]
    quarter = stored_grads.shape[1]
    dp_count = lax.axis_size("dp")
    tensor_count = lax.axis_size("tensor")
    sub_width = quarter // dp_count
    i = lax.axis_index("dp")
    dp_bits = bits_of(dp_count)
    tensor_bits = bits_of(tensor_count)

    rows = stored_grads[None]
    for bit in dp_bits[1:] + dp_bits[:1]:
        moved = swap(rows, "dp", bit)
        rows = jnp.concatenate([rows, moved], axis=0)
    cols = lax.dynamic_slice_in_dim(rows, i * sub_width, sub_width, 2)[None]
    offsets = [0]
    for bit in reversed(tensor_bits):
        moved = swap(cols, "tensor", bit)
        cols = jnp.concatenate([cols, moved], axis=0)
        offsets += [off ^ bit for off in offsets]

    total = project(
        inputs_x,
        hidden,
        grad_up,
        grad_down,
        proj_in_up,
        proj_in_down,
        proj_out_up,
        proj_out_down,
    )
    for bit in tensor_bits:
        other = swap(total, "tensor", bit)
        if bit != tensor_bits[-1]:
            total = total + other
    cur = current_rows(lengths, total, other, proj_width)
    cur = cur.reshape(1, examples, proj_width * LAYERS * proj_width)
    for bit in reversed(dp_bits):
        moved = swap(cur, "dp", bit)
        cur = jnp.concatenate([cur, moved], axis=0)
    product = gram(rows, cols, cur, offsets)
    return product.reshape(quarter, 1, tensor_count * sub_width)


def local_any(
    inputs_x,
    hidden,
    grad_up,
    grad_down,
    proj_in_up,
    proj_in_down,
    proj_out_up,
    proj_out_down,
    lengths,
    stored_grads,
):
    examples = lengths.shape[0]
    slot_count = inputs_x.shape[0] // examples
    proj_width = proj_in_up.shape[1]
    tensor_count = lax.axis_size("tensor")
    out_share = proj_width // tensor_count
    tensor_index = lax.axis_index("tensor")
    terms_in = jnp.stack([matmul(inputs_x, proj_in_up), matmul(hidden, proj_in_down)])
    terms_out = jnp.stack([matmul(grad_up, proj_out_up), matmul(grad_down, proj_out_down)])
    summed_in, summed_out = lax.psum((terms_in, terms_out), "tensor")
    summed_out = lax.dynamic_slice_in_dim(summed_out, tensor_index * out_share, out_share, 2)
    live_mask = (jnp.arange(slot_count, dtype=jnp.int32)[None, :] < lengths[:, None]).astype(
        jnp.float32
    )
    in_proj = summed_in.reshape(LAYERS, examples, slot_count, proj_width).transpose(1, 2, 0, 3)
    out_proj = summed_out.reshape(LAYERS, examples, slot_count, out_share).transpose(1, 2, 0, 3)
    out_proj = out_proj * live_mask[:, :, None, None]
    current = jnp.einsum("esla,eslb->ealb", out_proj, in_proj, precision=lax.Precision.HIGHEST)
    current = (current * (1.0 / math.sqrt(slot_count))).reshape(
        examples, out_share * LAYERS * proj_width
    )
    local_rows = jnp.concatenate([current.astype(jnp.bfloat16), stored_grads], axis=0)
    row_count = local_rows.shape[0]
    quarter = local_rows.shape[1]
    dp_count = lax.axis_size("dp")
    sub_width = quarter // dp_count
    every_count = row_count * dp_count
    everything = lax.all_gather(local_rows, "dp", axis=0, tiled=True)
    column_block = lax.dynamic_slice_in_dim(
        everything, lax.axis_index("dp") * sub_width, sub_width, 1
    )
    columns = lax.all_gather(column_block, "tensor", axis=1, tiled=True)
    product = lax.dot_general(
        everything, columns, (((0,), (0,)), ((), ())), preferred_element_type=jnp.float32
    )
    product = product * (1.0 / math.sqrt(every_count))
    return product.astype(jnp.bfloat16).reshape(quarter, 1, columns.shape[1])


def paired(dp_count, tensor_count, proj_width, quarter):
    sizes = power_of_two(dp_count) and power_of_two(tensor_count)
    many = dp_count > 1 and tensor_count > 1
    lanes = quarter % (dp_count * LANES) == 0 and LAYERS * proj_width == LANES
    return sizes and many and lanes


def solution(mesh):
    in_specs = (
        P("dp", "tensor"),
        P("dp", "tensor"),
        P("dp", "tensor"),
        P("dp", "tensor"),
        P("tensor", None),
        P("tensor", None),
        P("tensor", None),
        P("tensor", None),
        P("dp"),
        P("dp", "tensor"),
    )
    out_specs = P("tensor", "dp", None)

    def step(*args):
        counts = mesh.shape["dp"], mesh.shape["tensor"]
        quarter = args[9].shape[1] // counts[1]
        fits = paired(*counts, args[4].shape[1], quarter)
        body = local if fits else local_any
        return jax.shard_map(
            body, mesh=mesh, in_specs=in_specs, out_specs=out_specs, check_vma=False
        )(*args)

    return step
```

```python
import functools
import math

import jax
import jax.numpy as jnp
from jax import lax
from jax.experimental import pallas as pl
from jax.experimental.pallas import tpu as pltpu
from jax.sharding import PartitionSpec as P

LAYERS = 2
LANES = 128
SLOT = 16
MIB = 1 << 20


def matmul(left, right):
    return jnp.dot(left, right, preferred_element_type=jnp.float32)


def power_of_two(n):
    return n & (n - 1) == 0


def bits_of(n):
    return [1 << k for k in range(n.bit_length() - 1)]


def turned(bits):
    return bits[1:] + bits[:1]


def swap(value, axis, bit, odd_bit):
    dp_count, tensor_count = lax.axis_size("dp"), lax.axis_size("tensor")
    pairs = []
    for d in range(dp_count):
        by = odd_bit if d % 2 else bit
        for t in range(tensor_count):
            to = (d ^ by, t) if axis == "dp" else (d, t ^ by)
            pairs.append((d * tensor_count + t, to[0] * tensor_count + to[1]))
    return lax.ppermute(value, ("dp", "tensor"), pairs)


def project_kernel(x, h, gu, gd, pu, pd, ou, od, out, *scratch):
    ins = (x, h, gu, gd, pu, pd, ou, od)
    bufs, sem = scratch[:8], scratch[8]
    order = (4, 0, 7, 3, 5, 1, 6, 2)
    copies = {}
    for n in order:
        copies[n] = pltpu.make_async_copy(ins[n], bufs[n], sem.at[n])
        copies[n].start()

    def product(left, right):
        copies[right].wait()
        copies[left].wait()
        return lax.dot_general(
            bufs[left][...],
            bufs[right][...],
            (((1,), (1,)), ((), ())),
            preferred_element_type=jnp.float32,
        )

    rows = x.shape[0]
    in_up = product(0, 4)
    out_down = product(3, 7)
    in_down = product(1, 5)
    out[:rows, :] = jnp.concatenate([in_up, in_down], axis=1)
    out_up = product(2, 6)
    out[rows:, :] = jnp.concatenate([out_up, out_down], axis=1)


def project(x, h, gu, gd, pu, pd, ou, od):
    args = (x, h, gu, gd, pu.T, pd.T, ou.T, od.T)
    args = tuple(pltpu.with_memory_space_constraint(a, pltpu.HBM) for a in args)
    rows = x.shape[0]
    width = LAYERS * pu.shape[1]
    return pl.pallas_call(
        project_kernel,
        out_shape=jax.ShapeDtypeStruct((2 * rows, width), jnp.float32),
        in_specs=[pl.BlockSpec(memory_space=pltpu.HBM)] * 8,
        out_specs=pl.BlockSpec(memory_space=pltpu.VMEM),
        scratch_shapes=[pltpu.VMEM(a.shape, a.dtype) for a in args]
        + [pltpu.SemaphoreType.DMA((8,))],
        cost_estimate=pl.CostEstimate(
            flops=2 * sum(math.prod(a.shape) for a in args[:4]) * pu.shape[1],
            bytes_accessed=2 * sum(math.prod(a.shape) for a in args),
            transcendentals=0,
        ),
        compiler_params=pltpu.CompilerParams(vmem_limit_bytes=8 * MIB),
        name="project",
    )(*args)


def current_kernel(lengths, own, other, out):
    examples, half, width = out.shape
    total = own[...] + other[...]
    rows = total.shape[0] // 2
    slots = rows // examples
    position = lax.broadcasted_iota(jnp.int32, (slots, width), 0)
    lane = lax.broadcasted_iota(jnp.int32, (half, width), 1)
    for e in range(examples):
        left = total[rows + e * slots : rows + (e + 1) * slots]
        right = total[e * slots : (e + 1) * slots]
        left = left * (position < lengths[e]).astype(jnp.float32)
        both = lax.dot_general(
            left,
            right,
            (((0,), (0,)), ((), ())),
            precision=lax.Precision.HIGHEST,
            preferred_element_type=jnp.float32,
        )
        mine = jnp.where(lane < half, both[:half], both[half:])
        out[e] = (mine * (1.0 / math.sqrt(slots))).astype(out.dtype)


def current_rows(lengths, own, other, proj_width):
    examples = lengths.shape[0]
    return pl.pallas_call(
        current_kernel,
        out_shape=jax.ShapeDtypeStruct(
            (examples, proj_width, LAYERS * proj_width), jnp.bfloat16
        ),
        in_specs=[
            pl.BlockSpec(memory_space=pltpu.SMEM),
            pl.BlockSpec(memory_space=pltpu.VMEM),
            pl.BlockSpec(memory_space=pltpu.VMEM),
        ],
        out_specs=pl.BlockSpec(memory_space=pltpu.VMEM),
        cost_estimate=pl.CostEstimate(
            flops=2 * examples * 64 * width_flops(proj_width),
            bytes_accessed=own.size * 8,
            transcendentals=0,
        ),
        compiler_params=pltpu.CompilerParams(vmem_limit_bytes=4 * MIB),
        name="current",
    )(lengths, own, other)


def width_flops(proj_width):
    return (LAYERS * proj_width) ** 2


def gram_kernel(scale, offsets, stored, cols, cur, out, left, right, buf, sem):
    pieces, old, quarter = stored.shape
    new = cur.shape[1]
    sub = cols.shape[-1]
    slot = left.shape[0] // pieces
    q, i = lax.axis_index("tensor"), lax.axis_index("dp")
    left[...] = jnp.zeros_like(left)
    right[...] = jnp.zeros_like(right)
    for p in range(pieces):
        left[p * slot : p * slot + old, :] = stored[p]
        left[p * slot + old : p * slot + old + new, :] = cur[
            p, :, pl.ds(pl.multiple_of(q * quarter, quarter), quarter)
        ]
    for k, (even, odd) in enumerate(offsets):
        off = jnp.where(i % 2 == 0, even, odd)
        to = pl.multiple_of((q ^ off) * sub, sub)
        source = pl.multiple_of((q ^ off) * quarter + i * sub, sub)
        for p in range(pieces):
            right[p * slot : p * slot + old, pl.ds(to, sub)] = cols[k, p]
            right[p * slot + old : p * slot + old + new, pl.ds(to, sub)] = cur[
                p, :, pl.ds(source, sub)
            ]
    chunk = buf.shape[1]
    copies = []
    for m in range(buf.shape[0]):
        product = lax.dot_general(
            left[:, m * chunk : (m + 1) * chunk],
            right[...],
            (((0,), (0,)), ((), ())),
            preferred_element_type=jnp.float32,
        )
        buf[m] = (product * scale).astype(buf.dtype)
        copies.append(
            pltpu.make_async_copy(
                buf.at[m], out.at[pl.ds(m * chunk, chunk)], sem.at[m]
            )
        )
        copies[-1].start()
    for copy in copies:
        copy.wait()


def gram(stored, cols, cur, offsets):
    pieces, old, quarter = stored.shape
    new = cur.shape[1]
    slot = -(-(old + new) // SLOT) * SLOT
    width = cols.shape[0] * cols.shape[-1]
    chunk = 256 if quarter % 256 == 0 else quarter
    scale = 1.0 / math.sqrt(pieces * (old + new))
    return pl.pallas_call(
        functools.partial(gram_kernel, scale, offsets),
        out_shape=jax.ShapeDtypeStruct((quarter, width), jnp.bfloat16),
        in_specs=[pl.BlockSpec(memory_space=pltpu.VMEM)] * 3,
        out_specs=pl.BlockSpec(memory_space=pltpu.HBM),
        scratch_shapes=[
            pltpu.VMEM((pieces * slot, quarter), jnp.bfloat16),
            pltpu.VMEM((pieces * slot, width), jnp.bfloat16),
            pltpu.VMEM((quarter // chunk, chunk, width), jnp.bfloat16),
            pltpu.SemaphoreType.DMA((quarter // chunk,)),
        ],
        cost_estimate=pl.CostEstimate(
            flops=2 * pieces * slot * quarter * width,
            bytes_accessed=2 * quarter * width,
            transcendentals=0,
        ),
        compiler_params=pltpu.CompilerParams(vmem_limit_bytes=24 * MIB),
        name="gram",
    )(stored, cols, cur)


def local(
    inputs_x,
    hidden,
    grad_up,
    grad_down,
    proj_in_up,
    proj_in_down,
    proj_out_up,
    proj_out_down,
    lengths,
    stored_grads,
):
    examples = lengths.shape[0]
    proj_width = proj_in_up.shape[1]
    quarter = stored_grads.shape[1]
    dp_count = lax.axis_size("dp")
    tensor_count = lax.axis_size("tensor")
    sub_width = quarter // dp_count
    i = lax.axis_index("dp")
    links = bits_of(dp_count)[1:]
    dp_rounds = [*zip(links, turned(links), strict=True), (1, 1)]
    tensor_bits = bits_of(tensor_count)
    tensor_rounds = [*zip(tensor_bits, turned(tensor_bits), strict=True)]

    rows = stored_grads[None]
    for bits in dp_rounds:
        moved = swap(rows, "dp", *bits)
        rows = jnp.concatenate([rows, moved], axis=0)
    cols = lax.dynamic_slice_in_dim(rows, i * sub_width, sub_width, 2)[None]
    offsets = [(0, 0)]
    for bits in reversed(tensor_rounds):
        moved = swap(cols, "tensor", *bits)
        cols = jnp.concatenate([cols, moved], axis=0)
        offsets += [(even ^ bits[0], odd ^ bits[1]) for even, odd in offsets]

    total = project(
        inputs_x,
        hidden,
        grad_up,
        grad_down,
        proj_in_up,
        proj_in_down,
        proj_out_up,
        proj_out_down,
    )
    for n, bits in enumerate(tensor_rounds):
        other = swap(total, "tensor", *bits)
        if n < len(tensor_rounds) - 1:
            total = total + other
    cur = current_rows(lengths, total, other, proj_width)
    cur = cur.reshape(1, examples, proj_width * LAYERS * proj_width)
    for bits in dp_rounds:
        moved = swap(cur, "dp", *bits)
        cur = jnp.concatenate([cur, moved], axis=0)
    product = gram(rows, cols, cur, offsets)
    return product.reshape(quarter, 1, tensor_count * sub_width)


def local_any(
    inputs_x,
    hidden,
    grad_up,
    grad_down,
    proj_in_up,
    proj_in_down,
    proj_out_up,
    proj_out_down,
    lengths,
    stored_grads,
):
    examples = lengths.shape[0]
    slot_count = inputs_x.shape[0] // examples
    proj_width = proj_in_up.shape[1]
    tensor_count = lax.axis_size("tensor")
    out_share = proj_width // tensor_count
    tensor_index = lax.axis_index("tensor")
    terms_in = jnp.stack([matmul(inputs_x, proj_in_up), matmul(hidden, proj_in_down)])
    terms_out = jnp.stack([matmul(grad_up, proj_out_up), matmul(grad_down, proj_out_down)])
    summed_in, summed_out = lax.psum((terms_in, terms_out), "tensor")
    summed_out = lax.dynamic_slice_in_dim(summed_out, tensor_index * out_share, out_share, 2)
    live_mask = (jnp.arange(slot_count, dtype=jnp.int32)[None, :] < lengths[:, None]).astype(
        jnp.float32
    )
    in_proj = summed_in.reshape(LAYERS, examples, slot_count, proj_width).transpose(1, 2, 0, 3)
    out_proj = summed_out.reshape(LAYERS, examples, slot_count, out_share).transpose(1, 2, 0, 3)
    out_proj = out_proj * live_mask[:, :, None, None]
    current = jnp.einsum("esla,eslb->ealb", out_proj, in_proj, precision=lax.Precision.HIGHEST)
    current = (current * (1.0 / math.sqrt(slot_count))).reshape(
        examples, out_share * LAYERS * proj_width
    )
    local_rows = jnp.concatenate([current.astype(jnp.bfloat16), stored_grads], axis=0)
    row_count = local_rows.shape[0]
    quarter = local_rows.shape[1]
    dp_count = lax.axis_size("dp")
    sub_width = quarter // dp_count
    every_count = row_count * dp_count
    everything = lax.all_gather(local_rows, "dp", axis=0, tiled=True)
    column_block = lax.dynamic_slice_in_dim(
        everything, lax.axis_index("dp") * sub_width, sub_width, 1
    )
    columns = lax.all_gather(column_block, "tensor", axis=1, tiled=True)
    product = lax.dot_general(
        everything, columns, (((0,), (0,)), ((), ())), preferred_element_type=jnp.float32
    )
    product = product * (1.0 / math.sqrt(every_count))
    return product.astype(jnp.bfloat16).reshape(quarter, 1, columns.shape[1])


def paired(dp_count, tensor_count, proj_width, quarter):
    sizes = power_of_two(dp_count) and power_of_two(tensor_count)
    many = dp_count > 1 and tensor_count > 1
    lanes = quarter % (dp_count * LANES) == 0 and LAYERS * proj_width == LANES
    return sizes and many and lanes


def solution(mesh):
    in_specs = (
        P("dp", "tensor"),
        P("dp", "tensor"),
        P("dp", "tensor"),
        P("dp", "tensor"),
        P("tensor", None),
        P("tensor", None),
        P("tensor", None),
        P("tensor", None),
        P("dp"),
        P("dp", "tensor"),
    )
    out_specs = P("tensor", "dp", None)

    def step(*args):
        counts = mesh.shape["dp"], mesh.shape["tensor"]
        quarter = args[9].shape[1] // counts[1]
        fits = paired(*counts, args[4].shape[1], quarter)
        body = local if fits else local_any
        return jax.shard_map(
            body, mesh=mesh, in_specs=in_specs, out_specs=out_specs, check_vma=False
        )(*args)

    return step
```

```python
import functools
import math

import jax
import jax.numpy as jnp
from jax import lax
from jax.experimental import pallas as pl
from jax.experimental.pallas import tpu as pltpu
from jax.sharding import PartitionSpec as P

LAYERS = 2
LANES = 128
SLOT = 16
MIB = 1 << 20


def matmul(left, right):
    return jnp.dot(left, right, preferred_element_type=jnp.float32)


def power_of_two(n):
    return n & (n - 1) == 0


def bits_of(n):
    return [1 << k for k in range(n.bit_length() - 1)]


def turned(bits):
    return bits[1:] + bits[:1]


def swap(value, axis, bit, odd_bit):
    dp_count, tensor_count = lax.axis_size("dp"), lax.axis_size("tensor")
    pairs = []
    for d in range(dp_count):
        by = odd_bit if d % 2 else bit
        for t in range(tensor_count):
            to = (d ^ by, t) if axis == "dp" else (d, t ^ by)
            pairs.append((d * tensor_count + t, to[0] * tensor_count + to[1]))
    return lax.ppermute(value, ("dp", "tensor"), pairs)


def project_kernel(x, h, gu, gd, pu, pd, ou, od, stored, out, keep, *scratch):
    ins = (x, h, gu, gd, pu, pd, ou, od, stored)
    bufs, sem = (*scratch[:8], keep), scratch[8]
    order = (4, 0, 7, 3, 5, 1, 6, 2, 8)
    copies = {}
    for n in order:
        copies[n] = pltpu.make_async_copy(ins[n], bufs[n], sem.at[n])
        copies[n].start()

    def product(left, right):
        copies[right].wait()
        copies[left].wait()
        return lax.dot_general(
            bufs[left][...],
            bufs[right][...],
            (((1,), (1,)), ((), ())),
            preferred_element_type=jnp.float32,
        )

    rows = x.shape[0]
    in_up = product(0, 4)
    out_down = product(3, 7)
    in_down = product(1, 5)
    out[:rows, :] = jnp.concatenate([in_up, in_down], axis=1)
    out_up = product(2, 6)
    out[rows:, :] = jnp.concatenate([out_up, out_down], axis=1)
    copies[8].wait()


def project(x, h, gu, gd, pu, pd, ou, od, stored):
    args = (x, h, gu, gd, pu.T, pd.T, ou.T, od.T, stored)
    args = tuple(pltpu.with_memory_space_constraint(a, pltpu.HBM) for a in args)
    rows = x.shape[0]
    width = LAYERS * pu.shape[1]
    return pl.pallas_call(
        project_kernel,
        out_shape=(
            jax.ShapeDtypeStruct((2 * rows, width), jnp.float32),
            jax.ShapeDtypeStruct(stored.shape, stored.dtype),
        ),
        in_specs=[pl.BlockSpec(memory_space=pltpu.HBM)] * 9,
        out_specs=(pl.BlockSpec(memory_space=pltpu.VMEM),) * 2,
        scratch_shapes=[pltpu.VMEM(a.shape, a.dtype) for a in args[:8]]
        + [pltpu.SemaphoreType.DMA((9,))],
        cost_estimate=pl.CostEstimate(
            flops=2 * sum(math.prod(a.shape) for a in args[:4]) * pu.shape[1],
            bytes_accessed=2 * sum(math.prod(a.shape) for a in args),
            transcendentals=0,
        ),
        compiler_params=pltpu.CompilerParams(vmem_limit_bytes=8 * MIB),
        name="project",
    )(*args)


def current_kernel(lengths, own, other, out):
    examples, half, width = out.shape
    total = own[...] + other[...]
    rows = total.shape[0] // 2
    slots = rows // examples
    position = lax.broadcasted_iota(jnp.int32, (slots, width), 0)
    lane = lax.broadcasted_iota(jnp.int32, (half, width), 1)
    for e in range(examples):
        left = total[rows + e * slots : rows + (e + 1) * slots]
        right = total[e * slots : (e + 1) * slots]
        left = left * (position < lengths[e]).astype(jnp.float32)
        both = lax.dot_general(
            left,
            right,
            (((0,), (0,)), ((), ())),
            precision=lax.Precision.HIGHEST,
            preferred_element_type=jnp.float32,
        )
        mine = jnp.where(lane < half, both[:half], both[half:])
        out[e] = (mine * (1.0 / math.sqrt(slots))).astype(out.dtype)


def current_rows(lengths, own, other, proj_width):
    examples = lengths.shape[0]
    return pl.pallas_call(
        current_kernel,
        out_shape=jax.ShapeDtypeStruct(
            (examples, proj_width, LAYERS * proj_width), jnp.bfloat16
        ),
        in_specs=[
            pl.BlockSpec(memory_space=pltpu.SMEM),
            pl.BlockSpec(memory_space=pltpu.VMEM),
            pl.BlockSpec(memory_space=pltpu.VMEM),
        ],
        out_specs=pl.BlockSpec(memory_space=pltpu.VMEM),
        cost_estimate=pl.CostEstimate(
            flops=2 * examples * 64 * width_flops(proj_width),
            bytes_accessed=own.size * 8,
            transcendentals=0,
        ),
        compiler_params=pltpu.CompilerParams(vmem_limit_bytes=4 * MIB),
        name="current",
    )(lengths, own, other)


def width_flops(proj_width):
    return (LAYERS * proj_width) ** 2


def gram_kernel(scale, offsets, stored, cols, cur, moved, out, left, right, buf, sem):
    pieces, old, quarter = stored.shape
    half, new = cur.shape[:2]
    sub = cols.shape[-1]
    slot = left.shape[0] // pieces
    q, i = lax.axis_index("tensor"), lax.axis_index("dp")
    place = pl.ds(pl.multiple_of(q * quarter, quarter), quarter)
    left[...] = jnp.zeros_like(left)
    right[...] = jnp.zeros_like(right)
    for p in range(pieces):
        base = p * slot
        fresh = cur if p < half else moved
        left[base : base + old, :] = stored[p]
        left[base + old : base + old + new, :] = fresh[p % half, :, place]
    for block in range(len(offsets)):
        to = slice(block * sub, (block + 1) * sub)
        source = pl.ds(pl.multiple_of(block * quarter + i * sub, sub), sub)
        for p in range(pieces):
            base = p * slot + old
            fresh = cur if p < half else moved
            right[base : base + new, to] = fresh[p % half, :, source]
    for k, pair in enumerate(offsets):
        block = q ^ jnp.where(i % 2 == 0, *pair)
        to = pl.ds(pl.multiple_of(block * sub, sub), sub)
        for p in range(pieces):
            right[p * slot : p * slot + old, to] = cols[k, p]
    chunk = buf.shape[1]
    copies = []
    for m in range(buf.shape[0]):
        product = lax.dot_general(
            left[:, m * chunk : (m + 1) * chunk],
            right[...],
            (((0,), (0,)), ((), ())),
            preferred_element_type=jnp.float32,
        )
        buf[m] = (product * scale).astype(buf.dtype)
        copies.append(
            pltpu.make_async_copy(
                buf.at[m], out.at[pl.ds(m * chunk, chunk)], sem.at[m]
            )
        )
        copies[-1].start()
    for copy in copies:
        copy.wait()


def gram(stored, cols, cur, moved, offsets):
    pieces, old, quarter = stored.shape
    new = cur.shape[1]
    slot = -(-(old + new) // SLOT) * SLOT
    width = cols.shape[0] * cols.shape[-1]
    chunk = 256 if quarter % 256 == 0 else quarter
    scale = 1.0 / math.sqrt(pieces * (old + new))
    return pl.pallas_call(
        functools.partial(gram_kernel, scale, offsets),
        out_shape=jax.ShapeDtypeStruct((quarter, width), jnp.bfloat16),
        in_specs=[pl.BlockSpec(memory_space=pltpu.VMEM)] * 4,
        out_specs=pl.BlockSpec(memory_space=pltpu.HBM),
        scratch_shapes=[
            pltpu.VMEM((pieces * slot, quarter), jnp.bfloat16),
            pltpu.VMEM((pieces * slot, width), jnp.bfloat16),
            pltpu.VMEM((quarter // chunk, chunk, width), jnp.bfloat16),
            pltpu.SemaphoreType.DMA((quarter // chunk,)),
        ],
        cost_estimate=pl.CostEstimate(
            flops=2 * pieces * slot * quarter * width,
            bytes_accessed=2 * quarter * width,
            transcendentals=0,
        ),
        compiler_params=pltpu.CompilerParams(vmem_limit_bytes=24 * MIB),
        name="gram",
    )(stored, cols, cur, moved)


def local(
    inputs_x,
    hidden,
    grad_up,
    grad_down,
    proj_in_up,
    proj_in_down,
    proj_out_up,
    proj_out_down,
    lengths,
    stored_grads,
):
    examples = lengths.shape[0]
    proj_width = proj_in_up.shape[1]
    quarter = stored_grads.shape[1]
    dp_count = lax.axis_size("dp")
    tensor_count = lax.axis_size("tensor")
    sub_width = quarter // dp_count
    i = lax.axis_index("dp")
    links = bits_of(dp_count)[1:]
    dp_rounds = [*zip(links, turned(links), strict=True), (1, 1)]
    tensor_bits = bits_of(tensor_count)
    tensor_rounds = [*zip(tensor_bits, turned(tensor_bits), strict=True)]

    moved = swap(stored_grads, "dp", *dp_rounds[0])
    total, stored = project(
        inputs_x,
        hidden,
        grad_up,
        grad_down,
        proj_in_up,
        proj_in_down,
        proj_out_up,
        proj_out_down,
        stored_grads,
    )
    rows = jnp.stack([stored, moved])
    for n, bits in enumerate(dp_rounds[1:], 1):
        moved = swap(rows, "dp", *bits)
        rows = jnp.concatenate([rows, moved], axis=0)
    cols = lax.dynamic_slice_in_dim(rows, i * sub_width, sub_width, 2)[None]
    offsets = [(0, 0)]
    for bits in reversed(tensor_rounds):
        moved = swap(cols, "tensor", *bits)
        cols = jnp.concatenate([cols, moved], axis=0)
        offsets += [(even ^ bits[0], odd ^ bits[1]) for even, odd in offsets]

    for n, bits in enumerate(tensor_rounds):
        other = swap(total, "tensor", *bits)
        if n < len(tensor_rounds) - 1:
            total = total + other
    cur = current_rows(lengths, total, other, proj_width)
    cur = cur.reshape(1, examples, proj_width * LAYERS * proj_width)
    for n, bits in enumerate(dp_rounds):
        moved = swap(cur, "dp", *bits)
        if n < len(dp_rounds) - 1:
            cur = jnp.concatenate([cur, moved], axis=0)
    product = gram(rows, cols, cur, moved, offsets)
    return product.reshape(quarter, 1, tensor_count * sub_width)


def local_any(
    inputs_x,
    hidden,
    grad_up,
    grad_down,
    proj_in_up,
    proj_in_down,
    proj_out_up,
    proj_out_down,
    lengths,
    stored_grads,
):
    examples = lengths.shape[0]
    slot_count = inputs_x.shape[0] // examples
    proj_width = proj_in_up.shape[1]
    tensor_count = lax.axis_size("tensor")
    out_share = proj_width // tensor_count
    tensor_index = lax.axis_index("tensor")
    terms_in = jnp.stack([matmul(inputs_x, proj_in_up), matmul(hidden, proj_in_down)])
    terms_out = jnp.stack([matmul(grad_up, proj_out_up), matmul(grad_down, proj_out_down)])
    summed_in, summed_out = lax.psum((terms_in, terms_out), "tensor")
    summed_out = lax.dynamic_slice_in_dim(summed_out, tensor_index * out_share, out_share, 2)
    live_mask = (jnp.arange(slot_count, dtype=jnp.int32)[None, :] < lengths[:, None]).astype(
        jnp.float32
    )
    in_proj = summed_in.reshape(LAYERS, examples, slot_count, proj_width).transpose(1, 2, 0, 3)
    out_proj = summed_out.reshape(LAYERS, examples, slot_count, out_share).transpose(1, 2, 0, 3)
    out_proj = out_proj * live_mask[:, :, None, None]
    current = jnp.einsum("esla,eslb->ealb", out_proj, in_proj, precision=lax.Precision.HIGHEST)
    current = (current * (1.0 / math.sqrt(slot_count))).reshape(
        examples, out_share * LAYERS * proj_width
    )
    local_rows = jnp.concatenate([current.astype(jnp.bfloat16), stored_grads], axis=0)
    row_count = local_rows.shape[0]
    quarter = local_rows.shape[1]
    dp_count = lax.axis_size("dp")
    sub_width = quarter // dp_count
    every_count = row_count * dp_count
    everything = lax.all_gather(local_rows, "dp", axis=0, tiled=True)
    column_block = lax.dynamic_slice_in_dim(
        everything, lax.axis_index("dp") * sub_width, sub_width, 1
    )
    columns = lax.all_gather(column_block, "tensor", axis=1, tiled=True)
    product = lax.dot_general(
        everything, columns, (((0,), (0,)), ((), ())), preferred_element_type=jnp.float32
    )
    product = product * (1.0 / math.sqrt(every_count))
    return product.astype(jnp.bfloat16).reshape(quarter, 1, columns.shape[1])


def paired(dp_count, tensor_count, proj_width, quarter):
    sizes = power_of_two(dp_count) and power_of_two(tensor_count)
    many = dp_count > 1 and tensor_count > 1
    lanes = quarter % (dp_count * LANES) == 0 and LAYERS * proj_width == LANES
    return sizes and many and lanes


def solution(mesh):
    in_specs = (
        P("dp", "tensor"),
        P("dp", "tensor"),
        P("dp", "tensor"),
        P("dp", "tensor"),
        P("tensor", None),
        P("tensor", None),
        P("tensor", None),
        P("tensor", None),
        P("dp"),
        P("dp", "tensor"),
    )
    out_specs = P("tensor", "dp", None)

    def step(*args):
        counts = mesh.shape["dp"], mesh.shape["tensor"]
        quarter = args[9].shape[1] // counts[1]
        fits = paired(*counts, args[4].shape[1], quarter)
        body = local if fits else local_any
        return jax.shard_map(
            body, mesh=mesh, in_specs=in_specs, out_specs=out_specs, check_vma=False
        )(*args)

    return step
```

```python
import functools
import math

import jax
import jax.numpy as jnp
from jax import lax
from jax.experimental import pallas as pl
from jax.experimental.pallas import tpu as pltpu
from jax.sharding import PartitionSpec as P

LAYERS = 2
LANES = 128
SLOT = 16
MIB = 1 << 20


def matmul(left, right):
    return jnp.dot(left, right, preferred_element_type=jnp.float32)


def power_of_two(n):
    return n & (n - 1) == 0


def bits_of(n):
    return [1 << k for k in range(n.bit_length() - 1)]


def turned(bits):
    return bits[1:] + bits[:1]


def swap(value, axis, bit, odd_bit):
    dp_count, tensor_count = lax.axis_size("dp"), lax.axis_size("tensor")
    pairs = []
    for d in range(dp_count):
        by = odd_bit if d % 2 else bit
        for t in range(tensor_count):
            to = (d ^ by, t) if axis == "dp" else (d, t ^ by)
            pairs.append((d * tensor_count + t, to[0] * tensor_count + to[1]))
    return lax.ppermute(value, ("dp", "tensor"), pairs)


def project_kernel(x, h, gu, gd, pu, pd, ou, od, stored, out, keep, *scratch):
    ins = (x, h, gu, gd, pu, pd, ou, od, stored)
    bufs, sem = (*scratch[:8], keep), scratch[8]
    order = (4, 0, 7, 3, 5, 1, 6, 2, 8)
    copies = {}
    for n in order:
        copies[n] = pltpu.make_async_copy(ins[n], bufs[n], sem.at[n])
        copies[n].start()

    def product(left, right):
        copies[right].wait()
        copies[left].wait()
        return lax.dot_general(
            bufs[left][...],
            bufs[right][...],
            (((1,), (1,)), ((), ())),
            preferred_element_type=jnp.float32,
        )

    rows = x.shape[0]
    in_up = product(0, 4)
    out_down = product(3, 7)
    in_down = product(1, 5)
    out[:rows, :] = jnp.concatenate([in_up, in_down], axis=1)
    out_up = product(2, 6)
    out[rows:, :] = jnp.concatenate([out_up, out_down], axis=1)
    copies[8].wait()


def project(x, h, gu, gd, pu, pd, ou, od, stored):
    args = (x, h, gu, gd, pu.T, pd.T, ou.T, od.T, stored)
    args = tuple(pltpu.with_memory_space_constraint(a, pltpu.HBM) for a in args)
    rows = x.shape[0]
    width = LAYERS * pu.shape[1]
    return pl.pallas_call(
        project_kernel,
        out_shape=(
            jax.ShapeDtypeStruct((2 * rows, width), jnp.float32),
            jax.ShapeDtypeStruct(stored.shape, stored.dtype),
        ),
        in_specs=[pl.BlockSpec(memory_space=pltpu.HBM)] * 9,
        out_specs=(pl.BlockSpec(memory_space=pltpu.VMEM),) * 2,
        scratch_shapes=[pltpu.VMEM(a.shape, a.dtype) for a in args[:8]]
        + [pltpu.SemaphoreType.DMA((9,))],
        cost_estimate=pl.CostEstimate(
            flops=2 * sum(math.prod(a.shape) for a in args[:4]) * pu.shape[1],
            bytes_accessed=2 * sum(math.prod(a.shape) for a in args),
            transcendentals=0,
        ),
        compiler_params=pltpu.CompilerParams(vmem_limit_bytes=8 * MIB),
        name="project",
    )(*args)


def current_kernel(lengths, own, other, out):
    examples, half, width = out.shape
    total = own[...] + other[...]
    rows = total.shape[0] // 2
    slots = rows // examples
    position = lax.broadcasted_iota(jnp.int32, (slots, width), 0)
    lane = lax.broadcasted_iota(jnp.int32, (half, width), 1)
    for e in range(examples):
        left = total[rows + e * slots : rows + (e + 1) * slots]
        right = total[e * slots : (e + 1) * slots]
        left = left * (position < lengths[e]).astype(jnp.float32)
        both = lax.dot_general(
            left,
            right,
            (((0,), (0,)), ((), ())),
            precision=lax.Precision.HIGHEST,
            preferred_element_type=jnp.float32,
        )
        mine = jnp.where(lane < half, both[:half], both[half:])
        out[e] = (mine * (1.0 / math.sqrt(slots))).astype(out.dtype)


def current_rows(lengths, own, other, proj_width):
    examples = lengths.shape[0]
    return pl.pallas_call(
        current_kernel,
        out_shape=jax.ShapeDtypeStruct(
            (examples, proj_width, LAYERS * proj_width), jnp.bfloat16
        ),
        in_specs=[
            pl.BlockSpec(memory_space=pltpu.SMEM),
            pl.BlockSpec(memory_space=pltpu.VMEM),
            pl.BlockSpec(memory_space=pltpu.VMEM),
        ],
        out_specs=pl.BlockSpec(memory_space=pltpu.VMEM),
        cost_estimate=pl.CostEstimate(
            flops=2 * examples * 64 * width_flops(proj_width),
            bytes_accessed=own.size * 8,
            transcendentals=0,
        ),
        compiler_params=pltpu.CompilerParams(vmem_limit_bytes=4 * MIB),
        name="current",
    )(lengths, own, other)


def width_flops(proj_width):
    return (LAYERS * proj_width) ** 2


def gram_kernel(
    scale, offsets, stored, near, cols, cur, moved, out, left, right, buf, sem
):
    half, old, quarter = stored.shape
    pieces, new = 2 * half, cur.shape[1]
    sub = cols.shape[-1]
    slot = left.shape[0] // pieces
    q, i = lax.axis_index("tensor"), lax.axis_index("dp")
    place = pl.ds(pl.multiple_of(q * quarter, quarter), quarter)
    left[...] = jnp.zeros_like(left)
    right[...] = jnp.zeros_like(right)
    for p in range(pieces):
        base = p * slot
        here, fresh = (stored, cur) if p < half else (near, moved)
        left[base : base + old, :] = here[p % half]
        left[base + old : base + old + new, :] = fresh[p % half, :, place]
    for block in range(len(offsets)):
        to = slice(block * sub, (block + 1) * sub)
        source = pl.ds(pl.multiple_of(block * quarter + i * sub, sub), sub)
        for p in range(pieces):
            base = p * slot + old
            fresh = cur if p < half else moved
            right[base : base + new, to] = fresh[p % half, :, source]
    for k, pair in enumerate(offsets):
        block = q ^ jnp.where(i % 2 == 0, *pair)
        to = pl.ds(pl.multiple_of(block * sub, sub), sub)
        for p in range(pieces):
            right[p * slot : p * slot + old, to] = cols[k, p]
    chunk = buf.shape[1]
    copies = []
    for m in range(buf.shape[0]):
        product = lax.dot_general(
            left[:, m * chunk : (m + 1) * chunk],
            right[...],
            (((0,), (0,)), ((), ())),
            preferred_element_type=jnp.float32,
        )
        buf[m] = (product * scale).astype(buf.dtype)
        copies.append(
            pltpu.make_async_copy(
                buf.at[m], out.at[pl.ds(m * chunk, chunk)], sem.at[m]
            )
        )
        copies[-1].start()
    for copy in copies:
        copy.wait()


def gram(stored, near, cols, cur, moved, offsets):
    half, old, quarter = stored.shape
    pieces = 2 * half
    new = cur.shape[1]
    slot = -(-(old + new) // SLOT) * SLOT
    width = cols.shape[0] * cols.shape[-1]
    chunk = 256 if quarter % 256 == 0 else quarter
    scale = 1.0 / math.sqrt(pieces * (old + new))
    return pl.pallas_call(
        functools.partial(gram_kernel, scale, offsets),
        out_shape=jax.ShapeDtypeStruct((quarter, width), jnp.bfloat16),
        in_specs=[pl.BlockSpec(memory_space=pltpu.VMEM)] * 5,
        out_specs=pl.BlockSpec(memory_space=pltpu.HBM),
        scratch_shapes=[
            pltpu.VMEM((pieces * slot, quarter), jnp.bfloat16),
            pltpu.VMEM((pieces * slot, width), jnp.bfloat16),
            pltpu.VMEM((quarter // chunk, chunk, width), jnp.bfloat16),
            pltpu.SemaphoreType.DMA((quarter // chunk,)),
        ],
        cost_estimate=pl.CostEstimate(
            flops=2 * pieces * slot * quarter * width,
            bytes_accessed=2 * quarter * width,
            transcendentals=0,
        ),
        compiler_params=pltpu.CompilerParams(vmem_limit_bytes=24 * MIB),
        name="gram",
    )(stored, near, cols, cur, moved)


def local(
    inputs_x,
    hidden,
    grad_up,
    grad_down,
    proj_in_up,
    proj_in_down,
    proj_out_up,
    proj_out_down,
    lengths,
    stored_grads,
):
    examples = lengths.shape[0]
    proj_width = proj_in_up.shape[1]
    quarter = stored_grads.shape[1]
    dp_count = lax.axis_size("dp")
    tensor_count = lax.axis_size("tensor")
    sub_width = quarter // dp_count
    i = lax.axis_index("dp")
    links = bits_of(dp_count)[1:]
    dp_rounds = [*zip(links, turned(links), strict=True), (1, 1)]
    tensor_bits = bits_of(tensor_count)
    tensor_rounds = [*zip(tensor_bits, turned(tensor_bits), strict=True)]

    moved = swap(stored_grads, "dp", *dp_rounds[0])
    total, stored = project(
        inputs_x,
        hidden,
        grad_up,
        grad_down,
        proj_in_up,
        proj_in_down,
        proj_out_up,
        proj_out_down,
        stored_grads,
    )
    rows = jnp.stack([stored, moved])
    for n, bits in enumerate(dp_rounds[1:-1], 1):
        moved = swap(rows, "dp", *bits)
        rows = jnp.concatenate([rows, moved], axis=0)
    give = lax.dynamic_slice_in_dim(rows, (i ^ 1) * sub_width, sub_width, 2)
    got = swap(give, "dp", 1, 1)
    cols = lax.dynamic_slice_in_dim(rows, i * sub_width, sub_width, 2)
    cols = jnp.concatenate([cols, got], axis=0)[None]
    near = swap(rows, "dp", 1, 1)
    offsets = [(0, 0)]
    for bits in reversed(tensor_rounds):
        moved = swap(cols, "tensor", *bits)
        cols = jnp.concatenate([cols, moved], axis=0)
        offsets += [(even ^ bits[0], odd ^ bits[1]) for even, odd in offsets]

    for n, bits in enumerate(tensor_rounds):
        other = swap(total, "tensor", *bits)
        if n < len(tensor_rounds) - 1:
            total = total + other
    cur = current_rows(lengths, total, other, proj_width)
    cur = cur.reshape(1, examples, proj_width * LAYERS * proj_width)
    for n, bits in enumerate(dp_rounds):
        moved = swap(cur, "dp", *bits)
        if n < len(dp_rounds) - 1:
            cur = jnp.concatenate([cur, moved], axis=0)
    product = gram(rows, near, cols, cur, moved, offsets)
    return product.reshape(quarter, 1, tensor_count * sub_width)


def local_any(
    inputs_x,
    hidden,
    grad_up,
    grad_down,
    proj_in_up,
    proj_in_down,
    proj_out_up,
    proj_out_down,
    lengths,
    stored_grads,
):
    examples = lengths.shape[0]
    slot_count = inputs_x.shape[0] // examples
    proj_width = proj_in_up.shape[1]
    tensor_count = lax.axis_size("tensor")
    out_share = proj_width // tensor_count
    tensor_index = lax.axis_index("tensor")
    terms_in = jnp.stack([matmul(inputs_x, proj_in_up), matmul(hidden, proj_in_down)])
    terms_out = jnp.stack([matmul(grad_up, proj_out_up), matmul(grad_down, proj_out_down)])
    summed_in, summed_out = lax.psum((terms_in, terms_out), "tensor")
    summed_out = lax.dynamic_slice_in_dim(summed_out, tensor_index * out_share, out_share, 2)
    live_mask = (jnp.arange(slot_count, dtype=jnp.int32)[None, :] < lengths[:, None]).astype(
        jnp.float32
    )
    in_proj = summed_in.reshape(LAYERS, examples, slot_count, proj_width).transpose(1, 2, 0, 3)
    out_proj = summed_out.reshape(LAYERS, examples, slot_count, out_share).transpose(1, 2, 0, 3)
    out_proj = out_proj * live_mask[:, :, None, None]
    current = jnp.einsum("esla,eslb->ealb", out_proj, in_proj, precision=lax.Precision.HIGHEST)
    current = (current * (1.0 / math.sqrt(slot_count))).reshape(
        examples, out_share * LAYERS * proj_width
    )
    local_rows = jnp.concatenate([current.astype(jnp.bfloat16), stored_grads], axis=0)
    row_count = local_rows.shape[0]
    quarter = local_rows.shape[1]
    dp_count = lax.axis_size("dp")
    sub_width = quarter // dp_count
    every_count = row_count * dp_count
    everything = lax.all_gather(local_rows, "dp", axis=0, tiled=True)
    column_block = lax.dynamic_slice_in_dim(
        everything, lax.axis_index("dp") * sub_width, sub_width, 1
    )
    columns = lax.all_gather(column_block, "tensor", axis=1, tiled=True)
    product = lax.dot_general(
        everything, columns, (((0,), (0,)), ((), ())), preferred_element_type=jnp.float32
    )
    product = product * (1.0 / math.sqrt(every_count))
    return product.astype(jnp.bfloat16).reshape(quarter, 1, columns.shape[1])


def paired(dp_count, tensor_count, proj_width, quarter):
    sizes = power_of_two(dp_count) and power_of_two(tensor_count)
    many = dp_count > 1 and tensor_count > 1
    lanes = quarter % (dp_count * LANES) == 0 and LAYERS * proj_width == LANES
    return sizes and many and lanes


def solution(mesh):
    in_specs = (
        P("dp", "tensor"),
        P("dp", "tensor"),
        P("dp", "tensor"),
        P("dp", "tensor"),
        P("tensor", None),
        P("tensor", None),
        P("tensor", None),
        P("tensor", None),
        P("dp"),
        P("dp", "tensor"),
    )
    out_specs = P("tensor", "dp", None)

    def step(*args):
        counts = mesh.shape["dp"], mesh.shape["tensor"]
        quarter = args[9].shape[1] // counts[1]
        fits = paired(*counts, args[4].shape[1], quarter)
        body = local if fits else local_any
        return jax.shard_map(
            body, mesh=mesh, in_specs=in_specs, out_specs=out_specs, check_vma=False
        )(*args)

    return step
```

```python
import functools
import math

import jax
import jax.numpy as jnp
from jax import lax
from jax.experimental import pallas as pl
from jax.experimental.pallas import tpu as pltpu
from jax.sharding import PartitionSpec as P

LAYERS = 2
LANES = 128
SLOT = 16
MIB = 1 << 20


def matmul(left, right):
    return jnp.dot(left, right, preferred_element_type=jnp.float32)


def power_of_two(n):
    return n & (n - 1) == 0


def bits_of(n):
    return [1 << k for k in range(n.bit_length() - 1)]


def turned(bits):
    return bits[1:] + bits[:1]


def swap(value, axis, bit, odd_bit):
    dp_count, tensor_count = lax.axis_size("dp"), lax.axis_size("tensor")
    pairs = []
    for d in range(dp_count):
        by = odd_bit if d % 2 else bit
        for t in range(tensor_count):
            to = (d ^ by, t) if axis == "dp" else (d, t ^ by)
            pairs.append((d * tensor_count + t, to[0] * tensor_count + to[1]))
    return lax.ppermute(value, ("dp", "tensor"), pairs)


def project_kernel(x, h, gu, gd, pu, pd, ou, od, stored, out, keep, *scratch):
    ins = (x, h, gu, gd, pu, pd, ou, od, stored)
    bufs, sem = (*scratch[:8], keep), scratch[8]
    order = (4, 0, 7, 3, 5, 1, 6, 2, 8)
    copies = {}
    for n in order:
        copies[n] = pltpu.make_async_copy(ins[n], bufs[n], sem.at[n])
        copies[n].start()

    def product(left, right):
        copies[right].wait()
        copies[left].wait()
        return lax.dot_general(
            bufs[left][...],
            bufs[right][...],
            (((1,), (1,)), ((), ())),
            preferred_element_type=jnp.float32,
        )

    rows = x.shape[0]
    in_up = product(0, 4)
    out_down = product(3, 7)
    in_down = product(1, 5)
    out[:rows, :] = jnp.concatenate([in_up, in_down], axis=1)
    out_up = product(2, 6)
    out[rows:, :] = jnp.concatenate([out_up, out_down], axis=1)
    copies[8].wait()


def project(x, h, gu, gd, pu, pd, ou, od, stored):
    args = (x, h, gu, gd, pu.T, pd.T, ou.T, od.T, stored)
    args = tuple(pltpu.with_memory_space_constraint(a, pltpu.HBM) for a in args)
    rows = x.shape[0]
    width = LAYERS * pu.shape[1]
    return pl.pallas_call(
        project_kernel,
        out_shape=(
            jax.ShapeDtypeStruct((2 * rows, width), jnp.float32),
            jax.ShapeDtypeStruct(stored.shape, stored.dtype),
        ),
        in_specs=[pl.BlockSpec(memory_space=pltpu.HBM)] * 9,
        out_specs=(pl.BlockSpec(memory_space=pltpu.VMEM),) * 2,
        scratch_shapes=[pltpu.VMEM(a.shape, a.dtype) for a in args[:8]]
        + [pltpu.SemaphoreType.DMA((9,))],
        cost_estimate=pl.CostEstimate(
            flops=2 * sum(math.prod(a.shape) for a in args[:4]) * pu.shape[1],
            bytes_accessed=2 * sum(math.prod(a.shape) for a in args),
            transcendentals=0,
        ),
        compiler_params=pltpu.CompilerParams(vmem_limit_bytes=8 * MIB),
        name="project",
    )(*args)


def current_kernel(live, own, other, out):
    examples, half, width = out.shape
    total = own[...] + other[...]
    rows = total.shape[0] // 2
    slots = rows // examples
    lane = lax.broadcasted_iota(jnp.int32, (half, width), 1)
    for e in range(examples):
        left = total[rows + e * slots : rows + (e + 1) * slots]
        right = total[e * slots : (e + 1) * slots]
        left = left * live[e * slots : (e + 1) * slots, :]
        both = lax.dot_general(
            left,
            right,
            (((0,), (0,)), ((), ())),
            precision=lax.Precision.HIGHEST,
            preferred_element_type=jnp.float32,
        )
        mine = jnp.where(lane < half, both[:half], both[half:])
        out[e] = (mine * (1.0 / math.sqrt(slots))).astype(out.dtype)


def current_rows(lengths, own, other, proj_width):
    examples = lengths.shape[0]
    rows, width = own.shape[0] // 2, own.shape[1]
    position = lax.broadcasted_iota(jnp.int32, (examples, rows // examples, width), 1)
    live = (position < lengths[:, None, None]).astype(jnp.float32).reshape(rows, width)
    return pl.pallas_call(
        current_kernel,
        out_shape=jax.ShapeDtypeStruct(
            (examples, proj_width, LAYERS * proj_width), jnp.bfloat16
        ),
        in_specs=[pl.BlockSpec(memory_space=pltpu.VMEM)] * 3,
        out_specs=pl.BlockSpec(memory_space=pltpu.VMEM),
        cost_estimate=pl.CostEstimate(
            flops=2 * examples * 64 * width_flops(proj_width),
            bytes_accessed=own.size * 8,
            transcendentals=0,
        ),
        compiler_params=pltpu.CompilerParams(vmem_limit_bytes=4 * MIB),
        name="current",
    )(live, own, other)


def width_flops(proj_width):
    return (LAYERS * proj_width) ** 2


def fill(right, k, pair, cols, cur, moved, old):
    pieces, sub = cols.shape[0], cols.shape[-1]
    half, new = cur.shape[:2]
    slot = right.shape[0] // pieces
    q, i = lax.axis_index("tensor"), lax.axis_index("dp")
    quarter = cur.shape[-1] // lax.axis_size("tensor")
    block = q ^ jnp.where(i % 2 == 0, *pair)
    source = pl.ds(pl.multiple_of(block * quarter + i * sub, sub), sub)
    to = slice(k * sub, (k + 1) * sub)
    for p in range(pieces):
        base = p * slot
        fresh = cur if p < half else moved
        right[base : base + old, to] = cols[p]
        right[base + old : base + old + new, to] = fresh[p % half, :, source]
    return pl.ds(pl.multiple_of(block * sub, sub), sub)


def multiply(scale, left, right, places, out, buf, sem):
    chunk = buf.shape[2]
    copies = []
    for m in range(buf.shape[1]):
        product = lax.dot_general(
            left[:, m * chunk : (m + 1) * chunk],
            right[...],
            (((0,), (0,)), ((), ())),
            preferred_element_type=jnp.float32,
        )
        product = (product * scale).astype(buf.dtype)
        for k, place in enumerate(places):
            sub = buf.shape[3]
            buf[k, m] = product[:, k * sub : (k + 1) * sub]
            copies.append(
                pltpu.make_async_copy(
                    buf.at[k, m], out.at[pl.ds(m * chunk, chunk), place], sem.at[k, m]
                )
            )
            copies[-1].start()
    for copy in copies:
        copy.wait()


def gram_kernel(scale, offsets, stored, near, cur, moved, *refs):
    cols, (out, left, right, buf, sem) = refs[:-5], refs[-5:]
    half, old, quarter = stored.shape
    pieces, new = 2 * half, cur.shape[1]
    slot = left.shape[0] // pieces
    q = lax.axis_index("tensor")
    place = pl.ds(pl.multiple_of(q * quarter, quarter), quarter)
    left[...] = jnp.zeros_like(left)
    right[...] = jnp.zeros_like(right)
    for p in range(pieces):
        base = p * slot
        here, fresh = (stored, cur) if p < half else (near, moved)
        left[base : base + old, :] = here[p % half]
        left[base + old : base + old + new, :] = fresh[p % half, :, place]
    places = [
        fill(right, k, pair, cols[k], cur, moved, old) for k, pair in enumerate(offsets)
    ]
    multiply(scale, left, right, places, out, buf, sem)


def last_kernel(scale, offset, left, cur, moved, cols, begun, out, right, buf, sem):
    right[...] = jnp.zeros_like(right)
    place = fill(right, 0, offset, cols, cur, moved, cols.shape[1])
    multiply(scale, left, right, [place], out, buf, sem)


def gram(stored, near, cols, cur, moved, offsets):
    half, old, quarter = stored.shape
    pieces, new, sub = 2 * half, cur.shape[1], cols[0].shape[-1]
    slot = -(-(old + new) // SLOT) * SLOT
    depth, count = pieces * slot, len(cols)
    chunk = 256 if quarter % 256 == 0 else quarter
    scale = 1.0 / math.sqrt(pieces * (old + new))
    product = jax.ShapeDtypeStruct((quarter, count * sub), jnp.bfloat16)
    vmem, hbm = pl.BlockSpec(memory_space=pltpu.VMEM), pl.BlockSpec(memory_space=pltpu.HBM)

    def scratch(blocks):
        return [
            pltpu.VMEM((depth, blocks * sub), jnp.bfloat16),
            pltpu.VMEM((blocks, quarter // chunk, chunk, sub), jnp.bfloat16),
            pltpu.SemaphoreType.DMA((blocks, quarter // chunk)),
        ]

    def cost(blocks):
        return pl.CostEstimate(
            flops=2 * depth * quarter * blocks * sub,
            bytes_accessed=2 * quarter * blocks * sub,
            transcendentals=0,
        )

    params = pltpu.CompilerParams(vmem_limit_bytes=24 * MIB)
    begun, left = pl.pallas_call(
        functools.partial(gram_kernel, scale, offsets[:-1]),
        out_shape=(product, jax.ShapeDtypeStruct((depth, quarter), jnp.bfloat16)),
        in_specs=[vmem] * (3 + count),
        out_specs=(hbm, vmem),
        scratch_shapes=scratch(count - 1),
        cost_estimate=cost(count - 1),
        compiler_params=params,
        name="gram",
    )(stored, near, cur, moved, *cols[:-1])
    return pl.pallas_call(
        functools.partial(last_kernel, scale, offsets[-1]),
        out_shape=product,
        in_specs=[vmem] * 4 + [hbm],
        out_specs=hbm,
        scratch_shapes=scratch(1),
        input_output_aliases={4: 0},
        cost_estimate=cost(1),
        compiler_params=params,
        name="last",
    )(left, cur, moved, cols[-1], begun)


def local(
    inputs_x,
    hidden,
    grad_up,
    grad_down,
    proj_in_up,
    proj_in_down,
    proj_out_up,
    proj_out_down,
    lengths,
    stored_grads,
):
    examples = lengths.shape[0]
    proj_width = proj_in_up.shape[1]
    quarter = stored_grads.shape[1]
    dp_count = lax.axis_size("dp")
    tensor_count = lax.axis_size("tensor")
    sub_width = quarter // dp_count
    i = lax.axis_index("dp")
    links = bits_of(dp_count)[1:]
    dp_rounds = [*zip(links, turned(links), strict=True), (1, 1)]
    tensor_bits = bits_of(tensor_count)
    tensor_rounds = [*zip(tensor_bits, turned(tensor_bits), strict=True)]

    moved = swap(stored_grads, "dp", *dp_rounds[0])
    total, stored = project(
        inputs_x,
        hidden,
        grad_up,
        grad_down,
        proj_in_up,
        proj_in_down,
        proj_out_up,
        proj_out_down,
        stored_grads,
    )
    rows = jnp.stack([stored, moved])
    for n, bits in enumerate(dp_rounds[1:-1], 1):
        moved = swap(rows, "dp", *bits)
        rows = jnp.concatenate([rows, moved], axis=0)
    give = lax.dynamic_slice_in_dim(rows, (i ^ 1) * sub_width, sub_width, 2)
    got = swap(give, "dp", 1, 1)
    cols = lax.dynamic_slice_in_dim(rows, i * sub_width, sub_width, 2)
    cols = jnp.concatenate([cols, got], axis=0)
    near = swap(rows, "dp", 1, 1)
    first, second = reversed(tensor_rounds)
    beside = swap(cols, "tensor", *first)
    beyond = swap(cols, "tensor", *second)
    across = swap(beside, "tensor", *second)
    offsets = [(0, 0), first, second, (first[0] ^ second[0], first[1] ^ second[1])]
    cols = (cols, beside, beyond, across)

    for n, bits in enumerate(tensor_rounds):
        other = swap(total, "tensor", *bits)
        if n < len(tensor_rounds) - 1:
            total = total + other
    cur = current_rows(lengths, total, other, proj_width)
    cur = cur.reshape(1, examples, proj_width * LAYERS * proj_width)
    for n, bits in enumerate(dp_rounds):
        moved = swap(cur, "dp", *bits)
        if n < len(dp_rounds) - 1:
            cur = jnp.concatenate([cur, moved], axis=0)
    product = gram(rows, near, cols, cur, moved, offsets)
    return product.reshape(quarter, 1, tensor_count * sub_width)


def local_any(
    inputs_x,
    hidden,
    grad_up,
    grad_down,
    proj_in_up,
    proj_in_down,
    proj_out_up,
    proj_out_down,
    lengths,
    stored_grads,
):
    examples = lengths.shape[0]
    slot_count = inputs_x.shape[0] // examples
    proj_width = proj_in_up.shape[1]
    tensor_count = lax.axis_size("tensor")
    out_share = proj_width // tensor_count
    tensor_index = lax.axis_index("tensor")
    terms_in = jnp.stack([matmul(inputs_x, proj_in_up), matmul(hidden, proj_in_down)])
    terms_out = jnp.stack([matmul(grad_up, proj_out_up), matmul(grad_down, proj_out_down)])
    summed_in, summed_out = lax.psum((terms_in, terms_out), "tensor")
    summed_out = lax.dynamic_slice_in_dim(summed_out, tensor_index * out_share, out_share, 2)
    live_mask = (jnp.arange(slot_count, dtype=jnp.int32)[None, :] < lengths[:, None]).astype(
        jnp.float32
    )
    in_proj = summed_in.reshape(LAYERS, examples, slot_count, proj_width).transpose(1, 2, 0, 3)
    out_proj = summed_out.reshape(LAYERS, examples, slot_count, out_share).transpose(1, 2, 0, 3)
    out_proj = out_proj * live_mask[:, :, None, None]
    current = jnp.einsum("esla,eslb->ealb", out_proj, in_proj, precision=lax.Precision.HIGHEST)
    current = (current * (1.0 / math.sqrt(slot_count))).reshape(
        examples, out_share * LAYERS * proj_width
    )
    local_rows = jnp.concatenate([current.astype(jnp.bfloat16), stored_grads], axis=0)
    row_count = local_rows.shape[0]
    quarter = local_rows.shape[1]
    dp_count = lax.axis_size("dp")
    sub_width = quarter // dp_count
    every_count = row_count * dp_count
    everything = lax.all_gather(local_rows, "dp", axis=0, tiled=True)
    column_block = lax.dynamic_slice_in_dim(
        everything, lax.axis_index("dp") * sub_width, sub_width, 1
    )
    columns = lax.all_gather(column_block, "tensor", axis=1, tiled=True)
    product = lax.dot_general(
        everything, columns, (((0,), (0,)), ((), ())), preferred_element_type=jnp.float32
    )
    product = product * (1.0 / math.sqrt(every_count))
    return product.astype(jnp.bfloat16).reshape(quarter, 1, columns.shape[1])


def paired(dp_count, tensor_count, proj_width, quarter):
    sizes = power_of_two(dp_count) and power_of_two(tensor_count)
    many = dp_count > 1 and len(bits_of(tensor_count)) == 2
    lanes = quarter % (dp_count * LANES) == 0 and LAYERS * proj_width == LANES
    return sizes and many and lanes


def solution(mesh):
    in_specs = (
        P("dp", "tensor"),
        P("dp", "tensor"),
        P("dp", "tensor"),
        P("dp", "tensor"),
        P("tensor", None),
        P("tensor", None),
        P("tensor", None),
        P("tensor", None),
        P("dp"),
        P("dp", "tensor"),
    )
    out_specs = P("tensor", "dp", None)

    def step(*args):
        counts = mesh.shape["dp"], mesh.shape["tensor"]
        quarter = args[9].shape[1] // counts[1]
        fits = paired(*counts, args[4].shape[1], quarter)
        body = local if fits else local_any
        return jax.shard_map(
            body, mesh=mesh, in_specs=in_specs, out_specs=out_specs, check_vma=False
        )(*args)

    return step
```

```python
import functools
import math

import jax
import jax.numpy as jnp
from jax import lax
from jax.experimental import pallas as pl
from jax.experimental.pallas import tpu as pltpu
from jax.sharding import PartitionSpec as P

LAYERS = 2
LANES = 128
SLOT = 16
MIB = 1 << 20


def matmul(left, right):
    return jnp.dot(left, right, preferred_element_type=jnp.float32)


def power_of_two(n):
    return n & (n - 1) == 0


def bits_of(n):
    return [1 << k for k in range(n.bit_length() - 1)]


def turned(bits):
    return bits[1:] + bits[:1]


def swap(value, axis, bit, odd_bit):
    dp_count, tensor_count = lax.axis_size("dp"), lax.axis_size("tensor")
    pairs = []
    for d in range(dp_count):
        by = odd_bit if d % 2 else bit
        for t in range(tensor_count):
            to = (d ^ by, t) if axis == "dp" else (d, t ^ by)
            pairs.append((d * tensor_count + t, to[0] * tensor_count + to[1]))
    return lax.ppermute(value, ("dp", "tensor"), pairs)


def project_kernel(x, h, gu, gd, pu, pd, ou, od, stored, out, keep, *scratch):
    ins = (x, h, gu, gd, pu, pd, ou, od, stored)
    bufs, sem = (*scratch[:8], keep), scratch[8]
    order = (4, 0, 7, 3, 5, 1, 6, 2, 8)
    copies = {}
    for n in order:
        copies[n] = pltpu.make_async_copy(ins[n], bufs[n], sem.at[n])
        copies[n].start()

    def product(left, right):
        copies[right].wait()
        copies[left].wait()
        return lax.dot_general(
            bufs[left][...],
            bufs[right][...],
            (((1,), (1,)), ((), ())),
            preferred_element_type=jnp.float32,
        )

    rows = x.shape[0]
    in_up = product(0, 4)
    out_down = product(3, 7)
    in_down = product(1, 5)
    out[:rows, :] = jnp.concatenate([in_up, in_down], axis=1)
    out_up = product(2, 6)
    out[rows:, :] = jnp.concatenate([out_up, out_down], axis=1)
    copies[8].wait()


def project(x, h, gu, gd, pu, pd, ou, od, stored):
    args = (x, h, gu, gd, pu.T, pd.T, ou.T, od.T, stored)
    args = tuple(pltpu.with_memory_space_constraint(a, pltpu.HBM) for a in args)
    rows = x.shape[0]
    width = LAYERS * pu.shape[1]
    return pl.pallas_call(
        project_kernel,
        out_shape=(
            jax.ShapeDtypeStruct((2 * rows, width), jnp.float32),
            jax.ShapeDtypeStruct(stored.shape, stored.dtype),
        ),
        in_specs=[pl.BlockSpec(memory_space=pltpu.HBM)] * 9,
        out_specs=(pl.BlockSpec(memory_space=pltpu.VMEM),) * 2,
        scratch_shapes=[pltpu.VMEM(a.shape, a.dtype) for a in args[:8]]
        + [pltpu.SemaphoreType.DMA((9,))],
        cost_estimate=pl.CostEstimate(
            flops=2 * sum(math.prod(a.shape) for a in args[:4]) * pu.shape[1],
            bytes_accessed=2 * sum(math.prod(a.shape) for a in args),
            transcendentals=0,
        ),
        compiler_params=pltpu.CompilerParams(vmem_limit_bytes=8 * MIB),
        name="project",
    )(*args)


def current_kernel(live, own, other, out):
    examples, half, width = out.shape
    total = own[...] + other[...]
    rows = total.shape[0] // 2
    slots = rows // examples
    lane = lax.broadcasted_iota(jnp.int32, (half, width), 1)
    for e in range(examples):
        left = total[rows + e * slots : rows + (e + 1) * slots]
        right = total[e * slots : (e + 1) * slots]
        left = left * live[e * slots : (e + 1) * slots, :]
        both = lax.dot_general(
            left,
            right,
            (((0,), (0,)), ((), ())),
            precision=lax.Precision.HIGHEST,
            preferred_element_type=jnp.float32,
        )
        mine = jnp.where(lane < half, both[:half], both[half:])
        out[e] = (mine * (1.0 / math.sqrt(slots))).astype(out.dtype)


def current_rows(lengths, own, other, proj_width):
    examples = lengths.shape[0]
    rows, width = own.shape[0] // 2, own.shape[1]
    position = lax.broadcasted_iota(jnp.int32, (examples, rows // examples, width), 1)
    live = (position < lengths[:, None, None]).astype(jnp.float32).reshape(rows, width)
    return pl.pallas_call(
        current_kernel,
        out_shape=jax.ShapeDtypeStruct(
            (examples, proj_width, LAYERS * proj_width), jnp.bfloat16
        ),
        in_specs=[pl.BlockSpec(memory_space=pltpu.VMEM)] * 3,
        out_specs=pl.BlockSpec(memory_space=pltpu.VMEM),
        cost_estimate=pl.CostEstimate(
            flops=2 * examples * 64 * width_flops(proj_width),
            bytes_accessed=own.size * 8,
            transcendentals=0,
        ),
        compiler_params=pltpu.CompilerParams(vmem_limit_bytes=4 * MIB),
        name="current",
    )(live, own, other)


def width_flops(proj_width):
    return (LAYERS * proj_width) ** 2


def place_of(pair, sub):
    q, i = lax.axis_index("tensor"), lax.axis_index("dp")
    block = q ^ jnp.where(i % 2 == 0, *pair)
    return pl.ds(pl.multiple_of(block * sub, sub), sub)


def fill(right, k, pair, cols, cur, moved, old):
    pieces, sub = cols.shape[0], cols.shape[-1]
    half, new = cur.shape[:2]
    slot = right.shape[0] // pieces
    q, i = lax.axis_index("tensor"), lax.axis_index("dp")
    quarter = cur.shape[-1] // lax.axis_size("tensor")
    block = q ^ jnp.where(i % 2 == 0, *pair)
    source = pl.ds(pl.multiple_of(block * quarter + i * sub, sub), sub)
    to = slice(k * sub, (k + 1) * sub)
    for p in range(pieces):
        base = p * slot
        fresh = cur if p < half else moved
        right[base : base + old, to] = cols[p]
        right[base + old : base + old + new, to] = fresh[p % half, :, source]
    return pl.ds(pl.multiple_of(block * sub, sub), sub)


def multiply(scale, left, right, m, chunk, dtype):
    product = lax.dot_general(
        left[:, m * chunk : (m + 1) * chunk],
        right,
        (((0,), (0,)), ((), ())),
        preferred_element_type=jnp.float32,
    )
    return (product * scale).astype(dtype)


def send(source, out, m, place, sem):
    chunk = source.shape[0]
    copy = pltpu.make_async_copy(source, out.at[pl.ds(m * chunk, chunk), place], sem)
    copy.start()
    return copy


def gram_kernel(scale, offsets, stored, near, cur, moved, *refs):
    cols, (out, left, held, right, buf, sem) = refs[:-6], refs[-6:]
    half, old, quarter = stored.shape
    pieces, new = 2 * half, cur.shape[1]
    slot = left.shape[0] // pieces
    q = lax.axis_index("tensor")
    place = pl.ds(pl.multiple_of(q * quarter, quarter), quarter)
    left[...] = jnp.zeros_like(left)
    right[...] = jnp.zeros_like(right)
    for p in range(pieces):
        base = p * slot
        here, fresh = (stored, cur) if p < half else (near, moved)
        left[base : base + old, :] = here[p % half]
        left[base + old : base + old + new, :] = fresh[p % half, :, place]
    places = [
        fill(right, k, pair, cols[k], cur, moved, old) for k, pair in enumerate(offsets)
    ]
    count, steps, chunk, sub = buf.shape
    wide = count * sub
    copies = []
    for m in range(steps):
        product = multiply(scale, left, right[:, :wide], m, chunk, buf.dtype)
        for k in range(count):
            buf[k, m] = product[:, k * sub : (k + 1) * sub]
            copies.append(send(buf.at[k, m], out, m, places[k], sem.at[k, m]))
    for m in range(steps):
        held[m] = multiply(scale, left, right[:, wide:], m, chunk, held.dtype)
    for copy in copies:
        copy.wait()


def last_kernel(
    scale, offsets, left, held, cur, moved, cols, begun, out, right, buf, sem
):
    _, steps, chunk, sub = buf.shape
    place = place_of(offsets[0], sub)
    copies = [send(held.at[m], out, m, place, sem.at[0, m]) for m in range(steps)]
    right[...] = jnp.zeros_like(right)
    place = fill(right, 0, offsets[1], cols, cur, moved, cols.shape[1])
    for m in range(steps):
        buf[0, m] = multiply(scale, left, right[...], m, chunk, buf.dtype)
        copies.append(send(buf.at[0, m], out, m, place, sem.at[1, m]))
    for copy in copies:
        copy.wait()


def gram(stored, near, cols, cur, moved, offsets):
    half, old, quarter = stored.shape
    pieces, new, sub = 2 * half, cur.shape[1], cols[0].shape[-1]
    slot = -(-(old + new) // SLOT) * SLOT
    depth, count = pieces * slot, len(cols)
    chunk = 256 if quarter % 256 == 0 else quarter
    scale = 1.0 / math.sqrt(pieces * (old + new))
    product = jax.ShapeDtypeStruct((quarter, count * sub), jnp.bfloat16)
    vmem, hbm = pl.BlockSpec(memory_space=pltpu.VMEM), pl.BlockSpec(memory_space=pltpu.HBM)

    steps = quarter // chunk

    def scratch(blocks, kept, copies):
        return [
            pltpu.VMEM((depth, blocks * sub), jnp.bfloat16),
            pltpu.VMEM((kept, steps, chunk, sub), jnp.bfloat16),
            pltpu.SemaphoreType.DMA((copies, steps)),
        ]

    def cost(blocks):
        return pl.CostEstimate(
            flops=2 * depth * quarter * blocks * sub,
            bytes_accessed=2 * quarter * blocks * sub,
            transcendentals=0,
        )

    params = pltpu.CompilerParams(vmem_limit_bytes=24 * MIB)
    begun, left, held = pl.pallas_call(
        functools.partial(gram_kernel, scale, offsets[:-1]),
        out_shape=(
            product,
            jax.ShapeDtypeStruct((depth, quarter), jnp.bfloat16),
            jax.ShapeDtypeStruct((steps, chunk, sub), jnp.bfloat16),
        ),
        in_specs=[vmem] * (3 + count),
        out_specs=(hbm, vmem, vmem),
        scratch_shapes=scratch(count - 1, count - 2, count - 2),
        cost_estimate=cost(count - 1),
        compiler_params=params,
        name="gram",
    )(stored, near, cur, moved, *cols[:-1])
    return pl.pallas_call(
        functools.partial(last_kernel, scale, offsets[-2:]),
        out_shape=product,
        in_specs=[vmem] * 5 + [hbm],
        out_specs=hbm,
        scratch_shapes=scratch(1, 1, 2),
        input_output_aliases={5: 0},
        cost_estimate=cost(1),
        compiler_params=params,
        name="last",
    )(left, held, cur, moved, cols[-1], begun)


def local(
    inputs_x,
    hidden,
    grad_up,
    grad_down,
    proj_in_up,
    proj_in_down,
    proj_out_up,
    proj_out_down,
    lengths,
    stored_grads,
):
    examples = lengths.shape[0]
    proj_width = proj_in_up.shape[1]
    quarter = stored_grads.shape[1]
    dp_count = lax.axis_size("dp")
    tensor_count = lax.axis_size("tensor")
    sub_width = quarter // dp_count
    i = lax.axis_index("dp")
    links = bits_of(dp_count)[1:]
    dp_rounds = [*zip(links, turned(links), strict=True), (1, 1)]
    tensor_bits = bits_of(tensor_count)
    tensor_rounds = [*zip(tensor_bits, turned(tensor_bits), strict=True)]

    moved = swap(stored_grads, "dp", *dp_rounds[0])
    total, stored = project(
        inputs_x,
        hidden,
        grad_up,
        grad_down,
        proj_in_up,
        proj_in_down,
        proj_out_up,
        proj_out_down,
        stored_grads,
    )
    rows = jnp.stack([stored, moved])
    for n, bits in enumerate(dp_rounds[1:-1], 1):
        moved = swap(rows, "dp", *bits)
        rows = jnp.concatenate([rows, moved], axis=0)
    give = lax.dynamic_slice_in_dim(rows, (i ^ 1) * sub_width, sub_width, 2)
    got = swap(give, "dp", 1, 1)
    cols = lax.dynamic_slice_in_dim(rows, i * sub_width, sub_width, 2)
    cols = jnp.concatenate([cols, got], axis=0)
    near = swap(rows, "dp", 1, 1)
    first, second = reversed(tensor_rounds)
    beside = swap(cols, "tensor", *first)
    beyond = swap(cols, "tensor", *second)
    across = swap(beside, "tensor", *second)
    offsets = [(0, 0), first, second, (first[0] ^ second[0], first[1] ^ second[1])]
    cols = (cols, beside, beyond, across)

    for n, bits in enumerate(tensor_rounds):
        other = swap(total, "tensor", *bits)
        if n < len(tensor_rounds) - 1:
            total = total + other
    cur = current_rows(lengths, total, other, proj_width)
    cur = cur.reshape(1, examples, proj_width * LAYERS * proj_width)
    for n, bits in enumerate(dp_rounds):
        moved = swap(cur, "dp", *bits)
        if n < len(dp_rounds) - 1:
            cur = jnp.concatenate([cur, moved], axis=0)
    product = gram(rows, near, cols, cur, moved, offsets)
    return product.reshape(quarter, 1, tensor_count * sub_width)


def local_any(
    inputs_x,
    hidden,
    grad_up,
    grad_down,
    proj_in_up,
    proj_in_down,
    proj_out_up,
    proj_out_down,
    lengths,
    stored_grads,
):
    examples = lengths.shape[0]
    slot_count = inputs_x.shape[0] // examples
    proj_width = proj_in_up.shape[1]
    tensor_count = lax.axis_size("tensor")
    out_share = proj_width // tensor_count
    tensor_index = lax.axis_index("tensor")
    terms_in = jnp.stack([matmul(inputs_x, proj_in_up), matmul(hidden, proj_in_down)])
    terms_out = jnp.stack([matmul(grad_up, proj_out_up), matmul(grad_down, proj_out_down)])
    summed_in, summed_out = lax.psum((terms_in, terms_out), "tensor")
    summed_out = lax.dynamic_slice_in_dim(summed_out, tensor_index * out_share, out_share, 2)
    live_mask = (jnp.arange(slot_count, dtype=jnp.int32)[None, :] < lengths[:, None]).astype(
        jnp.float32
    )
    in_proj = summed_in.reshape(LAYERS, examples, slot_count, proj_width).transpose(1, 2, 0, 3)
    out_proj = summed_out.reshape(LAYERS, examples, slot_count, out_share).transpose(1, 2, 0, 3)
    out_proj = out_proj * live_mask[:, :, None, None]
    current = jnp.einsum("esla,eslb->ealb", out_proj, in_proj, precision=lax.Precision.HIGHEST)
    current = (current * (1.0 / math.sqrt(slot_count))).reshape(
        examples, out_share * LAYERS * proj_width
    )
    local_rows = jnp.concatenate([current.astype(jnp.bfloat16), stored_grads], axis=0)
    row_count = local_rows.shape[0]
    quarter = local_rows.shape[1]
    dp_count = lax.axis_size("dp")
    sub_width = quarter // dp_count
    every_count = row_count * dp_count
    everything = lax.all_gather(local_rows, "dp", axis=0, tiled=True)
    column_block = lax.dynamic_slice_in_dim(
        everything, lax.axis_index("dp") * sub_width, sub_width, 1
    )
    columns = lax.all_gather(column_block, "tensor", axis=1, tiled=True)
    product = lax.dot_general(
        everything, columns, (((0,), (0,)), ((), ())), preferred_element_type=jnp.float32
    )
    product = product * (1.0 / math.sqrt(every_count))
    return product.astype(jnp.bfloat16).reshape(quarter, 1, columns.shape[1])


def paired(dp_count, tensor_count, proj_width, quarter):
    sizes = power_of_two(dp_count) and power_of_two(tensor_count)
    many = dp_count > 1 and len(bits_of(tensor_count)) == 2
    lanes = quarter % (dp_count * LANES) == 0 and LAYERS * proj_width == LANES
    return sizes and many and lanes


def solution(mesh):
    in_specs = (
        P("dp", "tensor"),
        P("dp", "tensor"),
        P("dp", "tensor"),
        P("dp", "tensor"),
        P("tensor", None),
        P("tensor", None),
        P("tensor", None),
        P("tensor", None),
        P("dp"),
        P("dp", "tensor"),
    )
    out_specs = P("tensor", "dp", None)

    def step(*args):
        counts = mesh.shape["dp"], mesh.shape["tensor"]
        quarter = args[9].shape[1] // counts[1]
        fits = paired(*counts, args[4].shape[1], quarter)
        body = local if fits else local_any
        return jax.shard_map(
            body, mesh=mesh, in_specs=in_specs, out_specs=out_specs, check_vma=False
        )(*args)

    return step
```

```python
import functools
import math

import jax
import jax.numpy as jnp
from jax import lax
from jax.experimental import pallas as pl
from jax.experimental.pallas import tpu as pltpu
from jax.sharding import PartitionSpec as P

LAYERS = 2
LANES = 128
SLOT = 16
MIB = 1 << 20


def matmul(left, right):
    return jnp.dot(left, right, preferred_element_type=jnp.float32)


def power_of_two(n):
    return n & (n - 1) == 0


def bits_of(n):
    return [1 << k for k in range(n.bit_length() - 1)]


def turned(bits):
    return bits[1:] + bits[:1]


def swap(value, axis, bit, odd_bit):
    dp_count, tensor_count = lax.axis_size("dp"), lax.axis_size("tensor")
    pairs = []
    for d in range(dp_count):
        by = odd_bit if d % 2 else bit
        for t in range(tensor_count):
            to = (d ^ by, t) if axis == "dp" else (d, t ^ by)
            pairs.append((d * tensor_count + t, to[0] * tensor_count + to[1]))
    return lax.ppermute(value, ("dp", "tensor"), pairs)


def project_kernel(x, h, gu, gd, pu, pd, ou, od, stored, out, keep, *scratch):
    ins = (x, h, gu, gd, pu, pd, ou, od, stored)
    bufs, sem = (*scratch[:8], keep), scratch[8]
    order = (4, 0, 7, 3, 5, 1, 6, 2, 8)
    copies = {}
    for n in order:
        copies[n] = pltpu.make_async_copy(ins[n], bufs[n], sem.at[n])
        copies[n].start()

    def product(left, right):
        copies[right].wait()
        copies[left].wait()
        return lax.dot_general(
            bufs[left][...],
            bufs[right][...],
            (((1,), (1,)), ((), ())),
            preferred_element_type=jnp.float32,
        )

    rows = x.shape[0]
    in_up = product(0, 4)
    out_down = product(3, 7)
    in_down = product(1, 5)
    out[:rows, :] = jnp.concatenate([in_up, in_down], axis=1)
    out_up = product(2, 6)
    out[rows:, :] = jnp.concatenate([out_up, out_down], axis=1)
    copies[8].wait()


def project(x, h, gu, gd, pu, pd, ou, od, stored):
    args = (x, h, gu, gd, pu.T, pd.T, ou.T, od.T, stored)
    args = tuple(pltpu.with_memory_space_constraint(a, pltpu.HBM) for a in args)
    rows = x.shape[0]
    width = LAYERS * pu.shape[1]
    return pl.pallas_call(
        project_kernel,
        out_shape=(
            jax.ShapeDtypeStruct((2 * rows, width), jnp.float32),
            jax.ShapeDtypeStruct(stored.shape, stored.dtype),
        ),
        in_specs=[pl.BlockSpec(memory_space=pltpu.HBM)] * 9,
        out_specs=(pl.BlockSpec(memory_space=pltpu.VMEM),) * 2,
        scratch_shapes=[pltpu.VMEM(a.shape, a.dtype) for a in args[:8]]
        + [pltpu.SemaphoreType.DMA((9,))],
        cost_estimate=pl.CostEstimate(
            flops=2 * sum(math.prod(a.shape) for a in args[:4]) * pu.shape[1],
            bytes_accessed=2 * sum(math.prod(a.shape) for a in args),
            transcendentals=0,
        ),
        compiler_params=pltpu.CompilerParams(vmem_limit_bytes=8 * MIB),
        name="project",
    )(*args)


def current_kernel(rounds, live, own, other, out):
    examples, picked, width = out.shape
    total = own[...] + other[...]
    rows = total.shape[0] // 2
    slots = rows // examples
    half = width // LAYERS
    lane = lax.broadcasted_iota(jnp.int32, (half, width), 1)
    q, i = lax.axis_index("tensor"), lax.axis_index("dp")
    tensor_count, dp_count = lax.axis_size("tensor"), lax.axis_size("dp")
    share = half // tensor_count
    each, per_index = share // dp_count, half // dp_count
    place = lax.broadcasted_iota(jnp.int32, (picked, half), 0)
    later = jnp.maximum(place - share, 0)
    target, within = later // per_index, later % per_index
    index = jnp.zeros_like(place) + i
    for n, pair in enumerate(rounds):
        bit = jnp.where(i % 2 == 0, *pair)
        index = index ^ (((target >> (len(rounds) - 1 - n)) & 1) * bit)
    there = within // each * share + index * each + within % each
    vector = jnp.where(place < share, q * share + place, there)
    pick = (vector == lax.broadcasted_iota(jnp.int32, (picked, half), 1)).astype(out.dtype)
    for e in range(examples):
        left = total[rows + e * slots : rows + (e + 1) * slots]
        right = total[e * slots : (e + 1) * slots]
        left = left * live[e * slots : (e + 1) * slots, :]
        both = lax.dot_general(
            left,
            right,
            (((0,), (0,)), ((), ())),
            precision=lax.Precision.HIGHEST,
            preferred_element_type=jnp.float32,
        )
        mine = jnp.where(lane < half, both[:half], both[half:])
        mine = (mine * (1.0 / math.sqrt(slots))).astype(out.dtype)
        out[e] = matmul(pick, mine).astype(out.dtype)


def current_rows(lengths, own, other, proj_width, rounds):
    examples = lengths.shape[0]
    rows, width = own.shape[0] // 2, own.shape[1]
    picked = proj_width // lax.axis_size("tensor") + proj_width
    position = lax.broadcasted_iota(jnp.int32, (examples, rows // examples, width), 1)
    live = (position < lengths[:, None, None]).astype(jnp.float32).reshape(rows, width)
    return pl.pallas_call(
        functools.partial(current_kernel, rounds),
        out_shape=jax.ShapeDtypeStruct((examples, picked, width), jnp.bfloat16),
        in_specs=[pl.BlockSpec(memory_space=pltpu.VMEM)] * 3,
        out_specs=pl.BlockSpec(memory_space=pltpu.VMEM),
        cost_estimate=pl.CostEstimate(
            flops=2 * examples * 64 * width_flops(proj_width),
            bytes_accessed=own.size * 8,
            transcendentals=0,
        ),
        compiler_params=pltpu.CompilerParams(vmem_limit_bytes=4 * MIB),
        name="current",
    )(live, own, other)


def width_flops(proj_width):
    return (LAYERS * proj_width) ** 2


def place_of(pair, sub):
    q, i = lax.axis_index("tensor"), lax.axis_index("dp")
    block = q ^ jnp.where(i % 2 == 0, *pair)
    return pl.ds(pl.multiple_of(block * sub, sub), sub)


def fill(right, k, pair, cols, cur, moved, old):
    pieces, sub = cols.shape[0], cols.shape[-1]
    half, new = cur.shape[:2]
    slot = right.shape[0] // pieces
    q, i = lax.axis_index("tensor"), lax.axis_index("dp")
    quarter = sub * lax.axis_size("dp")
    block = q ^ jnp.where(i % 2 == 0, *pair)
    source = pl.ds(pl.multiple_of(quarter + block * sub, sub), sub)
    to = slice(k * sub, (k + 1) * sub)
    for p in range(pieces):
        base = p * slot
        fresh = cur if p < half else moved
        right[base : base + old, to] = cols[p]
        right[base + old : base + old + new, to] = fresh[p % half, :, source]
    return pl.ds(pl.multiple_of(block * sub, sub), sub)


def multiply(scale, left, right, m, chunk, dtype):
    product = lax.dot_general(
        left[:, m * chunk : (m + 1) * chunk],
        right,
        (((0,), (0,)), ((), ())),
        preferred_element_type=jnp.float32,
    )
    return (product * scale).astype(dtype)


def send(source, out, m, place, sem):
    chunk = source.shape[0]
    copy = pltpu.make_async_copy(source, out.at[pl.ds(m * chunk, chunk), place], sem)
    copy.start()
    return copy


def gram_kernel(scale, offsets, stored, near, cur, moved, *refs):
    cols, (out, left, held, right, buf, sem) = refs[:-6], refs[-6:]
    half, old, quarter = stored.shape
    pieces, new = 2 * half, cur.shape[1]
    slot = left.shape[0] // pieces
    left[...] = jnp.zeros_like(left)
    right[...] = jnp.zeros_like(right)
    for p in range(pieces):
        base = p * slot
        here, fresh = (stored, cur) if p < half else (near, moved)
        left[base : base + old, :] = here[p % half]
        left[base + old : base + old + new, :] = fresh[p % half, :, :quarter]
    places = [
        fill(right, k, pair, cols[k], cur, moved, old) for k, pair in enumerate(offsets)
    ]
    count, steps, chunk, sub = buf.shape
    wide = count * sub
    copies = []
    for m in range(steps):
        product = multiply(scale, left, right[:, :wide], m, chunk, buf.dtype)
        for k in range(count):
            buf[k, m] = product[:, k * sub : (k + 1) * sub]
            copies.append(send(buf.at[k, m], out, m, places[k], sem.at[k, m]))
    for m in range(steps):
        held[m] = multiply(scale, left, right[:, wide:], m, chunk, held.dtype)
    for copy in copies:
        copy.wait()


def last_kernel(
    scale, offsets, left, held, cur, moved, cols, begun, out, right, buf, sem
):
    _, steps, chunk, sub = buf.shape
    place = place_of(offsets[0], sub)
    copies = [send(held.at[m], out, m, place, sem.at[0, m]) for m in range(steps)]
    right[...] = jnp.zeros_like(right)
    place = fill(right, 0, offsets[1], cols, cur, moved, cols.shape[1])
    for m in range(steps):
        buf[0, m] = multiply(scale, left, right[...], m, chunk, buf.dtype)
        copies.append(send(buf.at[0, m], out, m, place, sem.at[1, m]))
    for copy in copies:
        copy.wait()


def gram(stored, near, cols, cur, moved, offsets):
    half, old, quarter = stored.shape
    pieces, new, sub = 2 * half, cur.shape[1], cols[0].shape[-1]
    slot = -(-(old + new) // SLOT) * SLOT
    depth, count = pieces * slot, len(cols)
    chunk = 256 if quarter % 256 == 0 else quarter
    scale = 1.0 / math.sqrt(pieces * (old + new))
    product = jax.ShapeDtypeStruct((quarter, count * sub), jnp.bfloat16)
    vmem, hbm = pl.BlockSpec(memory_space=pltpu.VMEM), pl.BlockSpec(memory_space=pltpu.HBM)

    steps = quarter // chunk

    def scratch(blocks, kept, copies):
        return [
            pltpu.VMEM((depth, blocks * sub), jnp.bfloat16),
            pltpu.VMEM((kept, steps, chunk, sub), jnp.bfloat16),
            pltpu.SemaphoreType.DMA((copies, steps)),
        ]

    def cost(blocks):
        return pl.CostEstimate(
            flops=2 * depth * quarter * blocks * sub,
            bytes_accessed=2 * quarter * blocks * sub,
            transcendentals=0,
        )

    params = pltpu.CompilerParams(vmem_limit_bytes=24 * MIB)
    begun, left, held = pl.pallas_call(
        functools.partial(gram_kernel, scale, offsets[:-1]),
        out_shape=(
            product,
            jax.ShapeDtypeStruct((depth, quarter), jnp.bfloat16),
            jax.ShapeDtypeStruct((steps, chunk, sub), jnp.bfloat16),
        ),
        in_specs=[vmem] * (3 + count),
        out_specs=(hbm, vmem, vmem),
        scratch_shapes=scratch(count - 1, count - 2, count - 2),
        cost_estimate=cost(count - 1),
        compiler_params=params,
        name="gram",
    )(stored, near, cur, moved, *cols[:-1])
    return pl.pallas_call(
        functools.partial(last_kernel, scale, offsets[-2:]),
        out_shape=product,
        in_specs=[vmem] * 5 + [hbm],
        out_specs=hbm,
        scratch_shapes=scratch(1, 1, 2),
        input_output_aliases={5: 0},
        cost_estimate=cost(1),
        compiler_params=params,
        name="last",
    )(left, held, cur, moved, cols[-1], begun)


def kept(cur, quarter):
    return (quarter + cur.shape[2]) // 2


def local(
    inputs_x,
    hidden,
    grad_up,
    grad_down,
    proj_in_up,
    proj_in_down,
    proj_out_up,
    proj_out_down,
    lengths,
    stored_grads,
):
    examples = lengths.shape[0]
    proj_width = proj_in_up.shape[1]
    quarter = stored_grads.shape[1]
    dp_count = lax.axis_size("dp")
    tensor_count = lax.axis_size("tensor")
    sub_width = quarter // dp_count
    i = lax.axis_index("dp")
    links = bits_of(dp_count)[1:]
    dp_rounds = [*zip(links, turned(links), strict=True), (1, 1)]
    fresh_rounds = [(bit, bit) for bit in links] + [(1, 1)]
    tensor_bits = bits_of(tensor_count)
    tensor_rounds = [*zip(tensor_bits, turned(tensor_bits), strict=True)]

    moved = swap(stored_grads, "dp", *dp_rounds[0])
    total, stored = project(
        inputs_x,
        hidden,
        grad_up,
        grad_down,
        proj_in_up,
        proj_in_down,
        proj_out_up,
        proj_out_down,
        stored_grads,
    )
    rows = jnp.stack([stored, moved])
    for n, bits in enumerate(dp_rounds[1:-1], 1):
        moved = swap(rows, "dp", *bits)
        rows = jnp.concatenate([rows, moved], axis=0)
    give = lax.dynamic_slice_in_dim(rows, (i ^ 1) * sub_width, sub_width, 2)
    got = swap(give, "dp", 1, 1)
    cols = lax.dynamic_slice_in_dim(rows, i * sub_width, sub_width, 2)
    cols = jnp.concatenate([cols, got], axis=0)
    near = swap(rows, "dp", 1, 1)
    first, second = reversed(tensor_rounds)
    beside = swap(cols, "tensor", *first)
    beyond = swap(cols, "tensor", *second)
    across = swap(beside, "tensor", *second)
    offsets = [(0, 0), first, second, (first[0] ^ second[0], first[1] ^ second[1])]
    cols = (cols, beside, beyond, across)

    for n, bits in enumerate(tensor_rounds):
        other = swap(total, "tensor", *bits)
        if n < len(tensor_rounds) - 1:
            total = total + other
    cur = current_rows(lengths, total, other, proj_width, fresh_rounds)
    cur = cur.reshape(1, examples, cur.shape[1] * cur.shape[2])
    give = jnp.concatenate([cur[..., :quarter], cur[..., kept(cur, quarter) :]], axis=2)
    for n, bits in enumerate(fresh_rounds):
        moved = swap(give, "dp", *bits)
        if n < len(dp_rounds) - 1:
            cur = jnp.concatenate([cur[..., : kept(cur, quarter)], moved], axis=0)
            give = jnp.concatenate([cur[..., :quarter], cur[..., kept(cur, quarter) :]], axis=2)
    product = gram(rows, near, cols, cur, moved, offsets)
    return product.reshape(quarter, 1, tensor_count * sub_width)


def local_any(
    inputs_x,
    hidden,
    grad_up,
    grad_down,
    proj_in_up,
    proj_in_down,
    proj_out_up,
    proj_out_down,
    lengths,
    stored_grads,
):
    examples = lengths.shape[0]
    slot_count = inputs_x.shape[0] // examples
    proj_width = proj_in_up.shape[1]
    tensor_count = lax.axis_size("tensor")
    out_share = proj_width // tensor_count
    tensor_index = lax.axis_index("tensor")
    terms_in = jnp.stack([matmul(inputs_x, proj_in_up), matmul(hidden, proj_in_down)])
    terms_out = jnp.stack([matmul(grad_up, proj_out_up), matmul(grad_down, proj_out_down)])
    summed_in, summed_out = lax.psum((terms_in, terms_out), "tensor")
    summed_out = lax.dynamic_slice_in_dim(summed_out, tensor_index * out_share, out_share, 2)
    live_mask = (jnp.arange(slot_count, dtype=jnp.int32)[None, :] < lengths[:, None]).astype(
        jnp.float32
    )
    in_proj = summed_in.reshape(LAYERS, examples, slot_count, proj_width).transpose(1, 2, 0, 3)
    out_proj = summed_out.reshape(LAYERS, examples, slot_count, out_share).transpose(1, 2, 0, 3)
    out_proj = out_proj * live_mask[:, :, None, None]
    current = jnp.einsum("esla,eslb->ealb", out_proj, in_proj, precision=lax.Precision.HIGHEST)
    current = (current * (1.0 / math.sqrt(slot_count))).reshape(
        examples, out_share * LAYERS * proj_width
    )
    local_rows = jnp.concatenate([current.astype(jnp.bfloat16), stored_grads], axis=0)
    row_count = local_rows.shape[0]
    quarter = local_rows.shape[1]
    dp_count = lax.axis_size("dp")
    sub_width = quarter // dp_count
    every_count = row_count * dp_count
    everything = lax.all_gather(local_rows, "dp", axis=0, tiled=True)
    column_block = lax.dynamic_slice_in_dim(
        everything, lax.axis_index("dp") * sub_width, sub_width, 1
    )
    columns = lax.all_gather(column_block, "tensor", axis=1, tiled=True)
    product = lax.dot_general(
        everything, columns, (((0,), (0,)), ((), ())), preferred_element_type=jnp.float32
    )
    product = product * (1.0 / math.sqrt(every_count))
    return product.astype(jnp.bfloat16).reshape(quarter, 1, columns.shape[1])


def paired(dp_count, tensor_count, proj_width, quarter):
    sizes = power_of_two(dp_count) and power_of_two(tensor_count)
    many = dp_count > 1 and len(bits_of(tensor_count)) == 2
    lanes = quarter % (dp_count * LANES) == 0 and LAYERS * proj_width == LANES
    return sizes and many and lanes


def solution(mesh):
    in_specs = (
        P("dp", "tensor"),
        P("dp", "tensor"),
        P("dp", "tensor"),
        P("dp", "tensor"),
        P("tensor", None),
        P("tensor", None),
        P("tensor", None),
        P("tensor", None),
        P("dp"),
        P("dp", "tensor"),
    )
    out_specs = P("tensor", "dp", None)

    def step(*args):
        counts = mesh.shape["dp"], mesh.shape["tensor"]
        quarter = args[9].shape[1] // counts[1]
        fits = paired(*counts, args[4].shape[1], quarter)
        body = local if fits else local_any
        return jax.shard_map(
            body, mesh=mesh, in_specs=in_specs, out_specs=out_specs, check_vma=False
        )(*args)

    return step
```
